256 devices in a mesh: px: 8 (over x, core), py: 32 (over z, y).
Axes of the slice: x: 4, y: 4, z: 8, core: 2. Of those that a mesh axis runs over, the one named last changes fastest.
Arguments:
- field: float32 [5, 64, 512, 128], P(None, 'px', 'py'), may hold values from -6 to 6
- forcing: float32 [5, 64, 512, 128], P(None, 'px', 'py'), may hold values from -6 to 6
- x_inverse: float32 [5, 5, 64, 512, 128], P(None, None, 'px', 'py'), may hold values from -1 to 1
- x_lower: float32 [5, 5, 64, 512, 128], P(None, None, 'px', 'py'), may hold values from -1 to 1
- x_upper: float32 [5, 5, 64, 512, 128], P(None, None, 'px', 'py'), may hold values from -1 to 1
- y_inverse: float32 [5, 5, 64, 512, 128], P(None, None, 'px', 'py'), may hold values from -1 to 1
- y_lower: float32 [5, 5, 64, 512, 128], P(None, None, 'px', 'py'), may hold values from -1 to 1
- y_upper: float32 [5, 5, 64, 512, 128], P(None, None, 'px', 'py'), may hold values from -1 to 1
Outputs:
- update: float32 [5, 64, 512, 128], P(None, 'px', 'py')
The draws below stay inside these ranges and needn't reach their ends.
All inputs are finite; a program needn't handle non-finite values.
Results may differ from the reference program's by a relative error of at most 0.00014.
Values sent between devices are 32-bit elements; how exact they have to be, the bound alone decides.
A program may use at most 64 MiB of HBM per device.

```python
import math
import jax
import jax.numpy as jnp
from jax import lax

NVAR = 5
NX = 64
NY = 512
NZ = 128


def coupling_block(key, line_dim, cells_per_line):
    array_extent = (NX, NY, NZ)
    line_shape = tuple((1 if k == line_dim else array_extent[k] for k in range(3)))
    random_keys = jax.random.split(key, 8)
    slow_share = 0.5
    slow = jax.random.bernoulli(random_keys[0], slow_share, (1,) + line_shape)
    spread = jnp.exp(jax.random.uniform(random_keys[1], (NVAR,) + array_extent, jnp.float32, math.log(0.6), math.log(1.6)))
    decay_rate = jnp.where(slow, 0.5 / cells_per_line, 3.0 / 40.0) * spread
    message_group = jax.random.bernoulli(random_keys[2], 3.0 / cells_per_line, (1,) + array_extent)
    damping_terms = jax.random.uniform(random_keys[3], (NVAR,) + array_extent, jnp.float32, 0.5, 0.8)
    retained_part = jnp.exp(-decay_rate) * jnp.where(message_group, damping_terms, 1.0)
    signs = jnp.where(jax.random.bernoulli(random_keys[5], 0.5, (2,) + array_extent), 1.0, -1.0)
    angles = jax.random.uniform(random_keys[4], (2,) + array_extent, jnp.float32, 0.4, 1.0) * signs
    cosine = jnp.cos(angles)
    sine = jnp.sin(angles)
    reflect_signs = jnp.where(jax.random.bernoulli(random_keys[6], 0.5, (NVAR,) + array_extent), 1.0, -1.0)
    reflect_axis = jax.random.uniform(random_keys[7], (NVAR,) + array_extent, jnp.float32, 0.5, 1.5) * reflect_signs
    norm_squared = jnp.sum(reflect_axis * reflect_axis, axis=0)
    unit_matrix = jnp.eye(NVAR, dtype=jnp.float32)[:, :, None, None, None]
    reflection = unit_matrix - 2.0 * reflect_axis[:, None] * reflect_axis[None, :] / norm_squared
    rows = [cosine[0] * reflection[0] - sine[0] * reflection[1], sine[0] * reflection[0] + cosine[0] * reflection[1], cosine[1] * reflection[2] - sine[1] * reflection[3], sine[1] * reflection[2] + cosine[1] * reflection[3], reflection[4]]
    matrix = jnp.stack(rows)
    return (retained_part[:, None] * matrix).astype(jnp.float32)


def inverse_block(key, cells_per_line):
    array_extent = (NX, NY, NZ)
    random_keys = jax.random.split(key, 2)
    lowest, highest = (0.5, 1.5)
    scales = jnp.exp(jax.random.uniform(random_keys[0], (NVAR, 1) + array_extent, jnp.float32, math.log(lowest), math.log(highest)))
    scales = scales * float(cells_per_line) ** (-0.75)
    mixing = jax.random.uniform(random_keys[1], (NVAR, NVAR) + array_extent, jnp.float32, -0.2, 0.2)
    unit_matrix = jnp.eye(NVAR, dtype=jnp.float32)[:, :, None, None, None]
    return (scales * (unit_matrix + mixing * (1.0 - unit_matrix))).astype(jnp.float32)


def draw_x_inverse(key, part):
    return inverse_block(jax.random.fold_in(key, 101), NX)


def draw_x_lower(key, part):
    return coupling_block(jax.random.fold_in(key, 102), 0, NX)


def draw_x_upper(key, part):
    return coupling_block(jax.random.fold_in(key, 103), 0, NX)


def draw_y_inverse(key, part):
    return inverse_block(jax.random.fold_in(key, 104), NY)


def draw_y_lower(key, part):
    return coupling_block(jax.random.fold_in(key, 105), 1, NY)


def draw_y_upper(key, part):
    return coupling_block(jax.random.fold_in(key, 106), 1, NY)


def level_of(rng, extent, shards, low, largest):
    gain, own = 1.0, jax.random.fold_in(rng, 6)
    for axis_at, parts in shards:
        draws = jnp.exp(jax.random.uniform(jax.random.fold_in(own, axis_at), (parts,), jnp.float32, low / len(shards), largest / len(shards)))
        gain = gain * jnp.repeat(draws, extent[axis_at] // parts).reshape([-1 if axis == axis_at else 1 for axis in range(len(extent))])
    return gain


def scatter_about(key, shape, deviation, most, cuts=(), kind=jnp.bfloat16):
    values = deviation * jax.random.normal(key, shape, jnp.float32)
    if cuts:
        values = values * level_of(key, shape, cuts, -0.22, 0.18)
    return jnp.clip(values, -most, most).astype(kind)


def setup_inputs(seed: int = 0) -> dict:
    streams_of = jax.random.split(jax.random.key(seed), 9)
    return {
        "field": scatter_about(streams_of[0], (NVAR, NX, NY, NZ), 1.0, 6.0, ((1, 8), (2, 32)), jnp.float32),
        "forcing": scatter_about(streams_of[1], (NVAR, NX, NY, NZ), 1.0, 6.0, ((1, 8), (2, 32)), jnp.float32),
        "x_inverse": draw_x_inverse(jax.random.fold_in(streams_of[8], 71), 0),
        "x_lower": draw_x_lower(jax.random.fold_in(streams_of[8], 71), 0),
        "x_upper": draw_x_upper(jax.random.fold_in(streams_of[8], 71), 0),
        "y_inverse": draw_y_inverse(jax.random.fold_in(streams_of[8], 71), 0),
        "y_lower": draw_y_lower(jax.random.fold_in(streams_of[8], 71), 0),
        "y_upper": draw_y_upper(jax.random.fold_in(streams_of[8], 71), 0),
    }


DISSIPATION = 0.1


def apply_block(blocks, vector):
    return jnp.sum(blocks * vector[None], axis=1)


def fourth_diff(values, line_axis):
    length = values.shape[line_axis]
    widths = [(0, 0)] * values.ndim
    widths[line_axis] = (2, 2)
    padded = jnp.pad(values, widths)

    def window(k):
        return lax.slice_in_dim(padded, k, k + length, axis=line_axis)

    return window(0) - 4.0 * window(1) + 6.0 * window(2) - 4.0 * window(3) + window(4)


def run_cells(source, coupling, inflow, line_axis, backward):
    length = source.shape[line_axis]

    def advance(i, carried):
        before, result = carried
        k = length - 1 - i if backward else i
        here = lax.dynamic_index_in_dim(coupling, k, line_axis + 1, keepdims=False)
        current = lax.dynamic_index_in_dim(source, k, line_axis, keepdims=False) - apply_block(here, before)
        return current, lax.dynamic_update_index_in_dim(result, current, k, line_axis)

    return lax.fori_loop(0, length, advance, (inflow, jnp.zeros_like(source)))[1]


def line_sweep(rhs, inverse, lower, upper, line_axis):
    source = apply_block(inverse, rhs)
    start = jnp.zeros(rhs.shape[:line_axis] + rhs.shape[line_axis + 1:], rhs.dtype)
    forward = run_cells(source, lower, start, line_axis, False)
    return run_cells(forward, upper, start, line_axis, True)


def reference(field, forcing, x_inverse, x_lower, x_upper, y_inverse, y_lower, y_upper):
    rhs = forcing - DISSIPATION * (fourth_diff(field, 1) + fourth_diff(field, 2))
    x_result = line_sweep(rhs, x_inverse, x_lower, x_upper, 1)
    return line_sweep(x_result, y_inverse, y_lower, y_upper, 2)
```

```python
import jax
import jax.numpy as jnp
from jax import lax
from jax.experimental import pallas as pl
from jax.experimental.pallas import tpu as pltpu
from jax.sharding import PartitionSpec as P

DISSIPATION = 0.1
MESH = pl.DeviceIdType.MESH
F32 = jnp.float32

V = 5
E = V * V
NPX, NPY, NPZ = 8, 32, 8
IN_Z = NPY // NPZ
CX, CY = 8, 16
ROWS = CX * CY
XM, YM = 76, 80
XV, YV = 12, 16
XO = CY // NPX


def block(ref, rows):
    return ref[:, rows, :].reshape(V, V, 8, 128)


def total(terms):
    while len(terms) > 1:
        terms = [terms[k] + terms[k + 1] if k + 1 < len(terms) else terms[k] for k in range(0, len(terms), 2)]
    return terms[0]


def apply(m, x):
    return total([m[:, c] * x[c][None] for c in range(V)])


def product(m, b):
    rows = [total([m[a, c][None] * b[c] for c in range(V)]) for a in range(V)]
    return jnp.stack(rows)


def device_products(lo, up, n, rows, psi, emit):
    first = block(lo, rows(0))
    psi[0] = first

    def forward(i, m):
        m = product(block(lo, rows(i)), m)
        psi[i] = m
        return m

    last = lax.fori_loop(1, n, forward, first)
    emit(0, last)

    def backward(t, z):
        i = n - 2 - t
        return psi[i] + product(block(up, rows(i)), z)

    emit(E, lax.fori_loop(0, n - 1, backward, last))

    def upward(t, m):
        return product(block(up, rows(n - 2 - t)), m)

    emit(2 * E, lax.fori_loop(0, n - 1, upward, block(up, rows(n - 1))))


def forward_cells(source, lo, rows, n, start, save):
    def step(i, carry):
        out = []
        for t, f in enumerate(carry):
            cur = source(i, t)
            if f is not None:
                cur = cur - apply(block(lo, rows(i, t)), f)
            save(i, t, cur)
            out.append(cur)
        return tuple(out)

    begin = 0
    if start[0] is None:
        start, begin = step(0, start), 1
    return lax.fori_loop(begin, n, step, start)


def backward_cells(source, up, rows, n, start, save):
    def step(k, carry):
        i = n - 1 - k
        out = []
        for t, g in enumerate(carry):
            cur = source(i, t)
            if g is not None:
                cur = cur - apply(block(up, rows(i, t)), g)
            if save is not None:
                save(i, t, cur)
            out.append(cur)
        return tuple(out)

    begin = 0
    if start[0] is None:
        start, begin = step(0, start), 1
    return lax.fori_loop(begin, n, step, start)


def kernel(field, forcing, xi, xl, xu, yi, yl, yu, out,
           fx, fo, xi_v, xl_v, xu_v, yi_v, yl_v, yu_v, res,
           fy, hx, hy, rhs, psi, sx, fwx, sy, fwy,
           xm_out, xm_in, xv_out, xv_in, xr_out, xr_in,
           ym_out, ym_in, yv_out, yv_in, yr_out, yr_in, xmat, ymat, cmat,
           load_s, halo_ss, halo_rs, xm_ss, xm_rs, xv_ss, xv_rs, xr_ss, xr_rs,
           ym_ss, ym_rs, yv_ss, yv_rs, yr_ss, yr_rs, out_s):
    px, py = lax.axis_index("px"), lax.axis_index("py")
    core, z = lax.rem(px, 2), lax.div(py, IN_Z)

    def owner_of(r):
        return IN_Z * r + lax.rem(2 * core + r, IN_Z)

    is_owner = py == owner_of(z)

    barrier = pltpu.get_barrier_semaphore()

    def greet_x(k, _):
        pl.semaphore_signal(barrier, inc=1, device_id=(lax.rem(px + k, NPX), py), device_id_type=MESH)
        return 0

    def greet_y(k, _):
        pl.semaphore_signal(barrier, inc=1, device_id=(px, lax.rem(py + k, NPY)), device_id_type=MESH)
        return 0

    lax.fori_loop(1, NPX, greet_x, 0)
    lax.fori_loop(1, NPY, greet_y, 0)

    mine = slice(2 * CY, 2 * CY + ROWS)
    loads = [
        pltpu.make_async_copy(a, b, load_s.at[k])
        for k, (a, b) in enumerate([
            (field, fx.at[:, mine, :]), (xl, xl_v), (xu, xu_v), (yl, yl_v), (yu, yu_v),
            (forcing, fo), (xi, xi_v), (yi, yi_v)])
    ]
    for c in loads:
        c.start()
    in_field, in_xl, in_xu, in_yl, in_yu, in_fo, in_xi, in_yi = loads

    def x_rows(i, h):
        return pl.ds(pl.multiple_of(CY * i + 8 * h, 8), 8)

    def y_rows(j, _=0):
        return pl.ds(j, 8, stride=CY)

    in_field.wait()

    def turn(j, _):
        fy[2 + j] = fx[:, pl.ds(2 * CY + j, 8, stride=CY), :]
        return 0

    lax.fori_loop(0, CY, turn, 0)

    in_xl.wait()
    in_xu.wait()
    for h in range(2):
        def emit(base, m, h=h):
            for e in range(E):
                xm_out[pl.ds(8 * h * XM + base + e, 8, stride=XM), :] = m[e // V, e % V]

        device_products(xl_v, xu_v, CX, lambda i, h=h: x_rows(i, h), psi, emit)

    pl.semaphore_wait(barrier, NPX + NPY - 2)

    right, left = lax.rem(px + 1, NPX), lax.rem(px + NPX - 1, NPX)
    north, south = lax.rem(py + 1, NPY), lax.rem(py + NPY - 1, NPY)
    halos = [
        pltpu.make_async_remote_copy(a, b, halo_ss.at[k], halo_rs.at[k], device_id=d, device_id_type=MESH)
        for k, (a, b, d) in enumerate([
            (fx.at[:, ROWS : ROWS + 2 * CY, :], hx.at[0], (right, py)),
            (fx.at[:, 2 * CY : 4 * CY, :], hx.at[1], (left, py)),
            (fy.at[CY : CY + 2], hy.at[0], (px, north)),
            (fy.at[2:4], hy.at[1], (px, south))])
    ]
    for c in halos:
        c.start()

    def at(ref, k, size):
        return ref.at[pl.ds(pl.multiple_of(k * size, 8), size), :]

    def x_copy(src, dst, ss, rs, size, k):
        return pltpu.make_async_remote_copy(
            at(src, k, size), at(dst, px, size), ss.at[k], rs.at[px], device_id=(k, py), device_id_type=MESH)

    def x_send(src, dst, ss, rs, size):
        pltpu.make_async_copy(at(src, px, size), at(dst, px, size), rs.at[px]).start()

        def one(k, _):
            x_copy(src, dst, ss, rs, size, lax.rem(px + k, NPX)).start()
            return 0

        lax.fori_loop(1, NPX, one, 0)

    def x_sent(src, dst, ss, rs, size):
        def one(k, _):
            x_copy(src, dst, ss, rs, size, lax.rem(px + k, NPX)).wait_send()
            return 0

        lax.fori_loop(1, NPX, one, 0)

    def received(dst, rs, size, count):
        def one(k, _):
            pltpu.make_async_copy(at(dst, k, size), at(dst, k, size), rs.at[k]).wait()
            return 0

        lax.fori_loop(0, count, one, 0)

    def y_copy(src, dst, ss, rs, size, r):
        return pltpu.make_async_remote_copy(
            at(src, r, size), at(dst, py, size), ss.at[r], rs.at[py], device_id=(px, owner_of(r)), device_id_type=MESH)

    def y_send(src, dst, ss, rs, size):
        @pl.when(is_owner)
        def _():
            pltpu.make_async_copy(at(src, z, size), at(dst, py, size), rs.at[py]).start()

        @pl.when(jnp.logical_not(is_owner))
        def _():
            y_copy(src, dst, ss, rs, size, z).start()

        def one(k, _):
            y_copy(src, dst, ss, rs, size, lax.rem(z + k, NPZ)).start()
            return 0

        lax.fori_loop(1, NPZ, one, 0)

    def y_sent(src, dst, ss, rs, size):
        @pl.when(jnp.logical_not(is_owner))
        def _():
            y_copy(src, dst, ss, rs, size, z).wait_send()

        def one(k, _):
            y_copy(src, dst, ss, rs, size, lax.rem(z + k, NPZ)).wait_send()
            return 0

        lax.fori_loop(1, NPZ, one, 0)

    xm = (xm_out, xm_in, xm_ss, xm_rs, XO * XM)
    xv = (xv_out, xv_in, xv_ss, xv_rs, XO * XV)
    xr = (xr_out, xr_in, xr_ss, xr_rs, XO * XV)
    ym = (ym_out, ym_in, ym_ss, ym_rs, YM)
    yv = (yv_out, yv_in, yv_ss, yv_rs, YV)
    x_send(*xm)

    in_yl.wait()
    in_yu.wait()

    def emit_y(base, m):
        for e in range(E):
            ym_out[pl.ds(base + e, 8, stride=YM), :] = m[e // V, e % V]

    device_products(yl_v, yu_v, CY, y_rows, psi, emit_y)
    y_send(*ym)

    in_fo.wait()
    for c in halos:
        c.wait()
    fx[:, 0 : 2 * CY, :] = jnp.where(px == 0, 0.0, hx[0])
    fx[:, 2 * CY + ROWS :, :] = jnp.where(px == NPX - 1, 0.0, hx[1])
    fy[0:2] = jnp.where(py == 0, 0.0, hy[0])
    fy[CY + 2 :] = jnp.where(py == NPY - 1, 0.0, hy[1])

    def difference(v):
        return v[0] - 4.0 * v[1] + 6.0 * v[2] - 4.0 * v[3] + v[4]

    def along_y(j, _):
        d = difference([fy[j + k] for k in range(5)])
        rhs[:, y_rows(j), :] = fo[:, y_rows(j), :] - DISSIPATION * d
        return 0

    lax.fori_loop(0, CY, along_y, 0)
    in_xi.wait()

    def x_source(i, h):
        d = difference([fx[:, x_rows(i + k, h), :] for k in range(5)])
        s = apply(block(xi_v, x_rows(i, h)), rhs[:, x_rows(i, h), :] - DISSIPATION * d)
        sx[:, x_rows(i, h), :] = s
        return s

    def save_fwx(i, h, f):
        fwx[:, x_rows(i, h), :] = f

    def load_fwx(i, h):
        return fwx[:, x_rows(i, h), :]

    ends = forward_cells(x_source, xl_v, x_rows, CX, (None, None), save_fwx)
    starts = backward_cells(load_fwx, xu_v, x_rows, CX, (None, None), None)
    for h in range(2):
        for c in range(V):
            xv_out[pl.ds(8 * h * XV + c, 8, stride=XV), :] = ends[h][c]
            xv_out[pl.ds(8 * h * XV + V + c, 8, stride=XV), :] = starts[h][c]
    x_send(*xv)

    place = lax.broadcasted_iota(jnp.int32, (V, 8, 128), 1)

    def chain(m, v):
        def one(_, a):
            return tuple(jnp.where(place == 0, 0.0, pltpu.roll(vk + apply(mk(), ak), 1, axis=1))
                         for vk, mk, ak in zip(v, m, a))

        return lax.fori_loop(0, 7, one, tuple(jnp.zeros((V, 8, 128), F32) for _ in v))

    def chain_back(m, v):
        def one(_, b):
            return tuple(jnp.where(place == 7, 0.0, pltpu.roll(vk + apply(mk(), bk), 7, axis=1))
                         for vk, mk, bk in zip(v, m, b))

        return lax.fori_loop(0, 7, one, tuple(jnp.zeros((V, 8, 128), F32) for _ in v))

    def held(ref, *at_):
        return lambda: ref[at_].reshape(V, V, 8, 128)

    received(xm_in, xm_rs, XO * XM, NPX)
    for r in range(XO):
        for e in range(3 * E):
            xmat[r, e // E, e % E] = xm_in[pl.ds(r * XM + e, 8, stride=XO * XM), :]
    received(xv_in, xv_rs, XO * XV, NPX)

    def rows_of(ref, first, stride):
        return jnp.stack([ref[pl.ds(first + c, 8, stride=stride), :] for c in range(V)])

    v = [rows_of(xv_in, r * XV, XO * XV) for r in range(XO)]
    w = [rows_of(xv_in, r * XV + V, XO * XV) for r in range(XO)]
    a = chain([held(xmat, r, 0) for r in range(XO)], v)
    w = [w[r] - apply(held(xmat, r, 1)(), a[r]) for r in range(XO)]
    b = chain_back([held(xmat, r, 2) for r in range(XO)], w)
    for r in range(XO):
        for c in range(V):
            xr_out[pl.ds(r * XV + c, 8, stride=XO * XV), :] = a[r][c]
            xr_out[pl.ds(r * XV + V + c, 8, stride=XO * XV), :] = b[r][c]
    x_send(*xr)
    received(xr_in, xr_rs, XO * XV, NPX)

    before = tuple(rows_of(xr_in, 8 * h * XV, XV) for h in range(2))
    after = tuple(rows_of(xr_in, 8 * h * XV + V, XV) for h in range(2))

    def load_sx(i, h):
        return sx[:, x_rows(i, h), :]

    forward_cells(load_sx, xl_v, x_rows, CX, before, save_fwx)
    backward_cells(load_fwx, xu_v, x_rows, CX, after, save_fwx)

    in_yi.wait()

    def y_source(j, _):
        s = apply(block(yi_v, y_rows(j)), fwx[:, y_rows(j), :])
        sy[j] = s
        return s

    def save_fwy(j, _, f):
        fwy[j] = f

    def load_fwy(j, _):
        return fwy[j]

    end, = forward_cells(y_source, yl_v, y_rows, CY, (None,), save_fwy)
    start, = backward_cells(load_fwy, yu_v, y_rows, CY, (None,), None)
    for c in range(V):
        yv_out[pl.ds(c, 8, stride=YV), :] = end[c]
        yv_out[pl.ds(V + c, 8, stride=YV), :] = start[c]
    y_send(*yv)

    def y_back(d):
        return pltpu.make_async_remote_copy(
            at(yr_out, d, YV), at(yr_in, z, YV), yr_ss.at[d], yr_rs.at[z], device_id=(px, d), device_id_type=MESH)

    @pl.when(is_owner)
    def _():
        received(ym_in, ym_rs, YM, NPY)
        for d in range(IN_Z):
            for e in range(3 * E):
                ymat[d, e // E, e % E] = ym_in[pl.ds(d * YM + e, 8, stride=IN_Z * YM), :]
        mm, mz, mn = [[held(ymat, d, k) for d in range(IN_Z)] for k in range(3)]

        def keep(k, m):
            cmat[k] = m.reshape(E, 8, 128)

        phi = mm[0]()
        x = []
        for d in range(1, IN_Z):
            keep(3 + d, product(mz[d](), phi))
            phi = product(mm[d](), phi)
        keep(0, phi)
        x = held(cmat, 3 + IN_Z - 1)()
        for d in range(IN_Z - 2, 0, -1):
            x = held(cmat, 3 + d)() + product(mn[d](), x)
        keep(1, mz[0]() + product(mn[0](), x))
        n = mn[IN_Z - 1]()
        for d in range(IN_Z - 2, -1, -1):
            n = product(mn[d](), n)
        keep(2, n)

        received(yv_in, yv_rs, YV, NPY)
        v = [rows_of(yv_in, d * YV, IN_Z * YV) for d in range(IN_Z)]
        w = [rows_of(yv_in, d * YV + V, IN_Z * YV) for d in range(IN_Z)]
        e = v[0]
        ins = [None]
        for d in range(1, IN_Z):
            ins.append(e)
            e = v[d] + apply(mm[d](), e)
        g = w[IN_Z - 1] - apply(mz[IN_Z - 1](), ins[IN_Z - 1])
        for d in range(IN_Z - 2, -1, -1):
            g = w[d] + apply(mn[d](), g)
            if d:
                g = g - apply(mz[d](), ins[d])
        a, = chain([held(cmat, 0)], [e])
        g = g - apply(held(cmat, 1)(), a)
        b, = chain_back([held(cmat, 2)], [g])
        ins = [a]
        for d in range(IN_Z - 1):
            ins.append(v[d] + apply(mm[d](), ins[d]))
        ahead = [None] * IN_Z
        ahead[IN_Z - 1] = b
        for d in range(IN_Z - 1, 0, -1):
            ahead[d - 1] = w[d] - apply(mz[d](), ins[d]) + apply(mn[d](), ahead[d])
        for d in range(IN_Z):
            for c in range(V):
                yr_out[pl.ds(d * YV + c, 8, stride=IN_Z * YV), :] = ins[d][c]
                yr_out[pl.ds(d * YV + V + c, 8, stride=IN_Z * YV), :] = ahead[d][c]

        pltpu.make_async_copy(at(yr_out, py, YV), at(yr_in, z, YV), yr_rs.at[z]).start()

        def one(k, _):
            y_back(lax.rem(py + k, NPY)).start()
            return 0

        lax.fori_loop(1, NPY, one, 0)

    received(yr_in, yr_rs, YV, NPZ)

    def load_sy(j, _):
        return sy[j]

    def save_res(j, _, u):
        res[:, y_rows(j), :] = u

    forward_cells(load_sy, yl_v, y_rows, CY, (rows_of(yr_in, 0, YV),), save_fwy)
    backward_cells(load_fwy, yu_v, y_rows, CY, (rows_of(yr_in, V, YV),), save_res)
    written = pltpu.make_async_copy(res, out, out_s.at[0])
    written.start()

    x_sent(*xm)
    x_sent(*xv)
    x_sent(*xr)
    y_sent(*ym)
    y_sent(*yv)

    @pl.when(is_owner)
    def _():
        def one(k, _):
            y_back(lax.rem(py + k, NPY)).wait_send()
            return 0

        lax.fori_loop(1, NPY, one, 0)

    written.wait()


def per_device(field, forcing, *blocks):
    shape = field.shape
    args = [v.reshape(V, ROWS, 128) for v in (field, forcing)] + [m.reshape(E, ROWS, 128) for m in blocks]

    def vmem(*dims):
        return pltpu.VMEM(dims, F32)

    def dma(n):
        return pltpu.SemaphoreType.DMA((n,))

    scratch = [
        vmem(V, ROWS + 4 * CY, 128), vmem(V, ROWS, 128), *[vmem(E, ROWS, 128) for _ in range(6)], vmem(V, ROWS, 128),
        vmem(CY + 4, V, 8, 128), vmem(2, V, 2 * CY, 128), vmem(2, 2, V, 8, 128), vmem(V, ROWS, 128),
        vmem(CY, V, V, 8, 128), vmem(V, ROWS, 128), vmem(V, ROWS, 128), vmem(CY, V, 8, 128), vmem(CY, V, 8, 128),
        vmem(CY * XM, 128), vmem(NPX * XO * XM, 128),
        vmem(CY * XV, 128), vmem(NPX * XO * XV, 128), vmem(NPX * XO * XV, 128), vmem(CY * XV, 128),
        vmem(CX * YM, 128), vmem(NPY * YM, 128), vmem(CX * YV, 128), vmem(NPY * YV, 128), vmem(NPY * YV, 128), vmem(CX * YV, 128),
        vmem(XO, 3, E, 8, 128), vmem(IN_Z, 3, E, 8, 128), vmem(3 + IN_Z, E, 8, 128),
        dma(8), dma(4), dma(4), dma(NPX), dma(NPX), dma(NPX), dma(NPX), dma(NPX), dma(NPX),
        dma(NPZ), dma(NPY), dma(NPZ), dma(NPY), dma(NPY), dma(NPZ), dma(1),
    ]
    result = pl.pallas_call(
        kernel,
        out_shape=jax.ShapeDtypeStruct((V, ROWS, 128), F32),
        in_specs=[pl.BlockSpec(memory_space=pl.ANY)] * 8,
        out_specs=pl.BlockSpec(memory_space=pl.ANY),
        scratch_shapes=scratch,
        compiler_params=pltpu.CompilerParams(collective_id=0, has_side_effects=True),
        name="adi",
    )(*args)
    return result.reshape(shape)


def solution(mesh):
    vector, matrix = P(None, "px", "py", None), P(None, None, "px", "py", None)
    return jax.shard_map(
        per_device, mesh=mesh, in_specs=(vector,) * 2 + (matrix,) * 6, out_specs=vector, check_vma=False
    )
```

```python
import jax
import jax.numpy as jnp
from jax import lax
from jax.experimental import pallas as pl
from jax.experimental.pallas import tpu as pltpu
from jax.sharding import PartitionSpec as P

DISSIPATION = 0.1
MESH = pl.DeviceIdType.MESH
F32 = jnp.float32

V = 5
E = V * V
NPX, NPY, NPZ = 8, 32, 8
IN_Z = NPY // NPZ
CX, CY = 8, 16
ROWS = CX * CY
XM, YM = 76, 80
XV, YV = 12, 16
YMP, YVP, YP = 88, 24, 24
XO = CY // NPX


def block(ref, rows):
    return ref[:, rows, :].reshape(V, V, 8, 128)


def total(terms):
    while len(terms) > 1:
        terms = [terms[k] + terms[k + 1] if k + 1 < len(terms) else terms[k] for k in range(0, len(terms), 2)]
    return terms[0]


def apply(m, x):
    return total([m[:, c] * x[c][None] for c in range(V)])


def product(m, b):
    rows = [total([m[a, c][None] * b[c] for c in range(V)]) for a in range(V)]
    return jnp.stack(rows)


def device_products(lo, up, up_again, n, psi, emit, before_up):
    first = lo(0)
    psi[0] = first

    def forward(i, m):
        m = product(lo(i), m)
        psi[i] = m
        return m

    last = lax.fori_loop(1, n, forward, first)
    emit(0, last)
    before_up()

    def backward(t, z):
        i = n - 2 - t
        return psi[i] + product(up(i), z)

    emit(E, lax.fori_loop(0, n - 1, backward, last))

    def upward(t, m):
        return product(up_again(n - 2 - t), m)

    emit(2 * E, lax.fori_loop(0, n - 1, upward, up(n - 1)))


def forward_cells(source, lo, n, start, save):
    def step(i, carry):
        out = []
        for t, f in enumerate(carry):
            cur = source(i, t)
            if f is not None:
                cur = cur - apply(lo(i, t), f)
            save(i, t, cur)
            out.append(cur)
        return tuple(out)

    begin = 0
    if start[0] is None:
        start, begin = step(0, start), 1
    return lax.fori_loop(begin, n, step, start)


def backward_cells(source, up, n, start, save):
    def step(k, carry):
        i = n - 1 - k
        out = []
        for t, g in enumerate(carry):
            cur = source(i, t)
            if g is not None:
                cur = cur - apply(up(i, t), g)
            if save is not None:
                save(i, t, cur)
            out.append(cur)
        return tuple(out)

    begin = 0
    if start[0] is None:
        start, begin = step(0, start), 1
    return lax.fori_loop(begin, n, step, start)


def kernel(field, forcing, xi, xl, xu, yi, yl, yu, out,
           fx, fo, xi_v, xl_v, xu_v, yi_v, yl_v, yu_v, yi_t, yl_t, yu_t,
           fy, hx, hy, rhs, psi, sx, fwx, sy, fwy,
           xm_out, xm_in, xv_out, xv_in, xr_out, xr_in,
           ym_out, ym_in, yv_out, yv_in, yr_out, yr_in, xmat, ymat, cmat,
           load_s, halo_ss, halo_rs, xm_ss, xm_rs, xv_ss, xv_rs, xr_ss, xr_rs,
           ym_ss, ym_rs, yv_ss, yv_rs, yr_ss, yr_rs):
    px, py = lax.axis_index("px"), lax.axis_index("py")
    core, z = lax.rem(px, 2), lax.div(py, IN_Z)

    def owner_of(r):
        return IN_Z * r + lax.rem(2 * core + r, IN_Z)

    is_owner = py == owner_of(z)

    mine = slice(2 * CY, 2 * CY + ROWS)

    def load(k, src, dst):
        return pltpu.make_async_copy(src, dst, load_s.at[k])

    padded = (slice(None), slice(None), slice(0, CY))
    in_xl, in_xu, in_field = load(0, xl, xl_v), load(1, xu, xu_v), load(2, field, fx.at[:, mine, :])
    in_yl, in_yu, in_yi = load(3, yl, yl_v.at[padded]), load(4, yu, yu_v.at[padded]), load(5, yi, yi_v.at[padded])
    in_fo, in_xi = load(6, forcing, fo), load(7, xi, xi_v)
    for c in (in_xl, in_xu, in_field):
        c.start()

    barrier = pltpu.get_barrier_semaphore()

    def greet_x(k, _):
        pl.semaphore_signal(barrier, inc=1, device_id=(lax.rem(px + k, NPX), py), device_id_type=MESH)
        return 0

    def greet_y(k, _):
        pl.semaphore_signal(barrier, inc=1, device_id=(px, lax.rem(py + k, NPY)), device_id_type=MESH)
        return 0

    lax.fori_loop(1, NPX, greet_x, 0)
    lax.fori_loop(1, NPY, greet_y, 0)

    def x_rows(i, h):
        return pl.ds(pl.multiple_of(CY * i + 8 * h, 8), 8)

    def y_rows(j):
        return pl.ds(j, 8, stride=CY)

    def turned(ref, j):
        return ref.reshape(E, CX * YP, 128)[:, pl.ds(j, 8, stride=YP), :].reshape(V, V, 8, 128)

    def x_block(ref):
        return lambda i, h: block(ref, x_rows(i, h))

    def y_block(ref):
        return lambda j, _=0: ref[j]

    def at(ref, k, size, pitch=None):
        return ref.at[pl.ds(pl.multiple_of(k * (pitch or size), 8), size), :]

    def x_copy(src, dst, ss, rs, size, k):
        return pltpu.make_async_remote_copy(
            at(src, k, size), at(dst, px, size), ss.at[k], rs.at[px], device_id=(k, py), device_id_type=MESH)

    def x_send_half(src, dst, ss, rs, size, half):
        first = 4 * half + lax.rem(px, 4)

        @pl.when(first == px)
        def _():
            pltpu.make_async_copy(at(src, px, size), at(dst, px, size), rs.at[px]).start()

        @pl.when(first != px)
        def _():
            x_copy(src, dst, ss, rs, size, first).start()

        for k in range(1, 4):
            x_copy(src, dst, ss, rs, size, 4 * half + lax.rem(px + k, 4)).start()

    def x_send(src, dst, ss, rs, size):
        pltpu.make_async_copy(at(src, px, size), at(dst, px, size), rs.at[px]).start()

        def one(k, _):
            x_copy(src, dst, ss, rs, size, lax.rem(px + k, NPX)).start()
            return 0

        lax.fori_loop(1, NPX, one, 0)

    def x_sent(src, dst, ss, rs, size):
        def one(k, _):
            x_copy(src, dst, ss, rs, size, lax.rem(px + k, NPX)).wait_send()
            return 0

        lax.fori_loop(1, NPX, one, 0)

    def received(dst, rs, size, count, pitch=None):
        def one(k, _):
            pltpu.make_async_copy(at(dst, k, size, pitch), at(dst, k, size, pitch), rs.at[k]).wait()
            return 0

        lax.fori_loop(0, count, one, 0)

    def slot(d):
        return NPZ * lax.rem(d, IN_Z) + lax.div(d, IN_Z)

    def y_copy(src, dst, ss, rs, size, pitch, r):
        return pltpu.make_async_remote_copy(
            at(src, r, size, pitch), at(dst, slot(py), size, pitch), ss.at[r], rs.at[slot(py)],
            device_id=(px, owner_of(r)), device_id_type=MESH)

    def y_send(src, dst, ss, rs, size, pitch):
        @pl.when(is_owner)
        def _():
            pltpu.make_async_copy(at(src, z, size, pitch), at(dst, slot(py), size, pitch), rs.at[slot(py)]).start()

        @pl.when(jnp.logical_not(is_owner))
        def _():
            y_copy(src, dst, ss, rs, size, pitch, z).start()

        def one(k, _):
            y_copy(src, dst, ss, rs, size, pitch, lax.rem(z + k, NPZ)).start()
            return 0

        lax.fori_loop(1, NPZ, one, 0)

    def y_sent(src, dst, ss, rs, size, pitch):
        @pl.when(jnp.logical_not(is_owner))
        def _():
            y_copy(src, dst, ss, rs, size, pitch, z).wait_send()

        def one(k, _):
            y_copy(src, dst, ss, rs, size, pitch, lax.rem(z + k, NPZ)).wait_send()
            return 0

        lax.fori_loop(1, NPZ, one, 0)

    xm = (xm_out, xm_in, xm_ss, xm_rs, XO * XM)
    xv = (xv_out, xv_in, xv_ss, xv_rs, XO * XV)
    xr = (xr_out, xr_in, xr_ss, xr_rs, XO * XV)
    ym = (ym_out, ym_in, ym_ss, ym_rs, YM, YMP)
    yv = (yv_out, yv_in, yv_ss, yv_rs, YV, YVP)
    in_field.wait()

    def turn(j, _):
        fy[2 + j] = fx[:, pl.ds(2 * CY + j, 8, stride=CY), :]
        return 0

    lax.fori_loop(0, CY, turn, 0)

    right, left = lax.rem(px + 1, NPX), lax.rem(px + NPX - 1, NPX)
    north, south = lax.rem(py + 1, NPY), lax.rem(py + NPY - 1, NPY)
    halos = [
        pltpu.make_async_remote_copy(a, b, halo_ss.at[k], halo_rs.at[k], device_id=d, device_id_type=MESH)
        for k, (a, b, d) in enumerate([
            (fx.at[:, ROWS : ROWS + 2 * CY, :], hx.at[0], (right, py)),
            (fx.at[:, 2 * CY : 4 * CY, :], hx.at[1], (left, py)),
            (fy.at[CY : CY + 2], hy.at[0], (px, north)),
            (fy.at[2:4], hy.at[1], (px, south))])
    ]
    in_xl.wait()
    in_yl.start()
    in_yu.start()
    for h in range(2):
        def emit(base, m, h=h):
            for e in range(E):
                xm_out[pl.ds(8 * h * XM + base + e, 8, stride=XM), :] = m[e // V, e % V]

        def before_up(h=h):
            if h == 0:
                in_xu.wait()
                for c in (in_fo, in_xi, in_yi):
                    c.start()

        lo, up = [lambda i, ref=ref, h=h: block(ref, x_rows(i, h)) for ref in (xl_v, xu_v)]
        device_products(lo, up, up, CX, psi, emit, before_up)
        if h == 0:
            pl.semaphore_wait(barrier, NPX + NPY - 2)
            for c in halos:
                c.start()
        x_send_half(*xm, h)

    in_yl.wait()

    def emit_y(base, m):
        for e in range(E):
            ym_out[pl.ds(base + e, 8, stride=YMP), :] = m[e // V, e % V]

    def lo_y(j):
        m = turned(yl_v, j)
        yl_t[j] = m
        return m

    def up_y(j):
        m = turned(yu_v, j)
        yu_t[j] = m
        return m

    device_products(lo_y, up_y, y_block(yu_t), CY, psi, emit_y, in_yu.wait)
    y_send(*ym)

    in_fo.wait()
    for c in halos:
        c.wait()
    fx[:, 0 : 2 * CY, :] = jnp.where(px == 0, 0.0, hx[0])
    fx[:, 2 * CY + ROWS :, :] = jnp.where(px == NPX - 1, 0.0, hx[1])
    fy[0:2] = jnp.where(py == 0, 0.0, hy[0])
    fy[CY + 2 :] = jnp.where(py == NPY - 1, 0.0, hy[1])

    def difference(v):
        return v[0] - 4.0 * v[1] + 6.0 * v[2] - 4.0 * v[3] + v[4]

    def along_y(j, _):
        d = difference([fy[j + k] for k in range(5)])
        rhs[:, y_rows(j), :] = fo[:, y_rows(j), :] - DISSIPATION * d
        return 0

    lax.fori_loop(0, CY, along_y, 0)
    in_xi.wait()

    def x_source(i, h):
        d = difference([fx[:, x_rows(i + k, h), :] for k in range(5)])
        s = apply(block(xi_v, x_rows(i, h)), rhs[:, x_rows(i, h), :] - DISSIPATION * d)
        sx[:, x_rows(i, h), :] = s
        return s

    def save_fwx(i, h, f):
        fwx[:, x_rows(i, h), :] = f

    def load_fwx(i, h):
        return fwx[:, x_rows(i, h), :]

    ends = forward_cells(x_source, x_block(xl_v), CX, (None, None), save_fwx)
    starts = backward_cells(load_fwx, x_block(xu_v), CX, (None, None), None)
    for h in range(2):
        for c in range(V):
            xv_out[pl.ds(8 * h * XV + c, 8, stride=XV), :] = ends[h][c]
            xv_out[pl.ds(8 * h * XV + V + c, 8, stride=XV), :] = starts[h][c]
    x_send(*xv)

    place = lax.broadcasted_iota(jnp.int32, (V, 8, 128), 1)

    def chain(m, v):
        def one(_, a):
            return tuple(jnp.where(place == 0, 0.0, pltpu.roll(vk + apply(mk(), ak), 1, axis=1))
                         for vk, mk, ak in zip(v, m, a))

        return lax.fori_loop(0, 7, one, tuple(jnp.zeros((V, 8, 128), F32) for _ in v))

    def chain_back(m, v):
        def one(_, b):
            return tuple(jnp.where(place == 7, 0.0, pltpu.roll(vk + apply(mk(), bk), 7, axis=1))
                         for vk, mk, bk in zip(v, m, b))

        return lax.fori_loop(0, 7, one, tuple(jnp.zeros((V, 8, 128), F32) for _ in v))

    def held(ref, *at_):
        return lambda: ref[at_].reshape(V, V, 8, 128)

    in_yi.wait()

    def turn_yi(j, _):
        yi_t[j] = turned(yi_v, j)
        return 0

    lax.fori_loop(0, CY, turn_yi, 0)

    received(xm_in, xm_rs, XO * XM, NPX)
    for r in range(XO):
        for e in range(3 * E):
            xmat[r, e // E, e % E] = xm_in[pl.ds(r * XM + e, 8, stride=XO * XM), :]
    received(xv_in, xv_rs, XO * XV, NPX)

    def rows_of(ref, first, stride):
        return jnp.stack([ref[pl.ds(first + c, 8, stride=stride), :] for c in range(V)])

    v = [rows_of(xv_in, r * XV, XO * XV) for r in range(XO)]
    w = [rows_of(xv_in, r * XV + V, XO * XV) for r in range(XO)]
    a = chain([held(xmat, r, 0) for r in range(XO)], v)
    w = [w[r] - apply(held(xmat, r, 1)(), a[r]) for r in range(XO)]
    b = chain_back([held(xmat, r, 2) for r in range(XO)], w)
    for r in range(XO):
        for c in range(V):
            xr_out[pl.ds(r * XV + c, 8, stride=XO * XV), :] = a[r][c]
            xr_out[pl.ds(r * XV + V + c, 8, stride=XO * XV), :] = b[r][c]
    x_send(*xr)
    received(xr_in, xr_rs, XO * XV, NPX)

    before = tuple(rows_of(xr_in, 8 * h * XV, XV) for h in range(2))
    after = tuple(rows_of(xr_in, 8 * h * XV + V, XV) for h in range(2))

    def load_sx(i, h):
        return sx[:, x_rows(i, h), :]

    forward_cells(load_sx, x_block(xl_v), CX, before, save_fwx)
    backward_cells(load_fwx, x_block(xu_v), CX, after, save_fwx)

    def y_source(j, _):
        s = apply(yi_t[j], fwx[:, y_rows(j), :])
        sy[j] = s
        return s

    def save_fwy(j, _, f):
        fwy[j] = f

    def load_fwy(j, _):
        return fwy[j]

    end, = forward_cells(y_source, y_block(yl_t), CY, (None,), save_fwy)
    start, = backward_cells(load_fwy, y_block(yu_t), CY, (None,), None)
    for c in range(V):
        yv_out[pl.ds(c, 8, stride=YVP), :] = end[c]
        yv_out[pl.ds(V + c, 8, stride=YVP), :] = start[c]
    y_send(*yv)

    def y_back(d):
        return pltpu.make_async_remote_copy(
            at(yr_out, slot(d), YV, YVP), at(yr_in, z, YV, YVP), yr_ss.at[d], yr_rs.at[z], device_id=(px, d), device_id_type=MESH)

    @pl.when(is_owner)
    def _():
        received(ym_in, ym_rs, YM, NPY, YMP)
        for d in range(IN_Z):
            for e in range(3 * E):
                ymat[d, e // E, e % E] = ym_in[pl.ds(d * NPZ * YMP + e, 8, stride=YMP), :]
        mm, mz, mn = [[held(ymat, d, k) for d in range(IN_Z)] for k in range(3)]

        def keep(k, m):
            cmat[k] = m.reshape(E, 8, 128)

        phi = mm[0]()
        x = []
        for d in range(1, IN_Z):
            keep(3 + d, product(mz[d](), phi))
            phi = product(mm[d](), phi)
        keep(0, phi)
        x = held(cmat, 3 + IN_Z - 1)()
        for d in range(IN_Z - 2, 0, -1):
            x = held(cmat, 3 + d)() + product(mn[d](), x)
        keep(1, mz[0]() + product(mn[0](), x))
        n = mn[IN_Z - 1]()
        for d in range(IN_Z - 2, -1, -1):
            n = product(mn[d](), n)
        keep(2, n)

        received(yv_in, yv_rs, YV, NPY, YVP)
        v = [rows_of(yv_in, d * NPZ * YVP, YVP) for d in range(IN_Z)]
        w = [rows_of(yv_in, d * NPZ * YVP + V, YVP) for d in range(IN_Z)]
        e = v[0]
        ins = [None]
        for d in range(1, IN_Z):
            ins.append(e)
            e = v[d] + apply(mm[d](), e)
        g = w[IN_Z - 1] - apply(mz[IN_Z - 1](), ins[IN_Z - 1])
        for d in range(IN_Z - 2, -1, -1):
            g = w[d] + apply(mn[d](), g)
            if d:
                g = g - apply(mz[d](), ins[d])
        a, = chain([held(cmat, 0)], [e])
        g = g - apply(held(cmat, 1)(), a)
        b, = chain_back([held(cmat, 2)], [g])
        ins = [a]
        for d in range(IN_Z - 1):
            ins.append(v[d] + apply(mm[d](), ins[d]))
        ahead = [None] * IN_Z
        ahead[IN_Z - 1] = b
        for d in range(IN_Z - 1, 0, -1):
            ahead[d - 1] = w[d] - apply(mz[d](), ins[d]) + apply(mn[d](), ahead[d])
        for d in range(IN_Z):
            for c in range(V):
                yr_out[pl.ds(d * NPZ * YVP + c, 8, stride=YVP), :] = ins[d][c]
                yr_out[pl.ds(d * NPZ * YVP + V + c, 8, stride=YVP), :] = ahead[d][c]

        pltpu.make_async_copy(at(yr_out, slot(py), YV, YVP), at(yr_in, z, YV, YVP), yr_rs.at[z]).start()

        def one(k, _):
            y_back(lax.rem(py + k, NPY)).start()
            return 0

        lax.fori_loop(1, NPY, one, 0)

    received(yr_in, yr_rs, YV, NPZ, YVP)

    def load_sy(j, _):
        return sy[j]

    def save_res(j, _, u):
        out[:, y_rows(j), :] = u

    forward_cells(load_sy, y_block(yl_t), CY, (rows_of(yr_in, 0, YVP),), save_fwy)
    backward_cells(load_fwy, y_block(yu_t), CY, (rows_of(yr_in, V, YVP),), save_res)

    x_sent(*xm)
    x_sent(*xv)
    x_sent(*xr)
    y_sent(*ym)
    y_sent(*yv)

    @pl.when(is_owner)
    def _():
        def one(k, _):
            y_back(lax.rem(py + k, NPY)).wait_send()
            return 0

        lax.fori_loop(1, NPY, one, 0)


def per_device(field, forcing, *blocks):
    shape = field.shape
    args = [v.reshape(V, ROWS, 128) for v in (field, forcing)] + [m.reshape(E, ROWS, 128) for m in blocks[:3]]
    args += [m.reshape(E, CX, CY, 128) for m in blocks[3:]]

    def vmem(*dims):
        return pltpu.VMEM(dims, F32)

    def dma(n):
        return pltpu.SemaphoreType.DMA((n,))

    scratch = [
        vmem(V, ROWS + 4 * CY, 128), vmem(V, ROWS, 128), *[vmem(E, ROWS, 128) for _ in range(3)],
        *[vmem(E, CX, YP, 128) for _ in range(3)], *[vmem(CY, V, V, 8, 128) for _ in range(3)],
        vmem(CY + 4, V, 8, 128), vmem(2, V, 2 * CY, 128), vmem(2, 2, V, 8, 128), vmem(V, ROWS, 128),
        vmem(CY, V, V, 8, 128), vmem(V, ROWS, 128), vmem(V, ROWS, 128), vmem(CY, V, 8, 128), vmem(CY, V, 8, 128),
        vmem(CY * XM, 128), vmem(NPX * XO * XM, 128),
        vmem(CY * XV, 128), vmem(NPX * XO * XV, 128), vmem(NPX * XO * XV, 128), vmem(CY * XV, 128),
        vmem(CX * YMP, 128), vmem(NPY * YMP, 128),
        vmem(CX * YVP, 128), vmem(NPY * YVP, 128), vmem(NPY * YVP, 128), vmem(CX * YVP, 128),
        vmem(XO, 3, E, 8, 128), vmem(IN_Z, 3, E, 8, 128), vmem(3 + IN_Z, E, 8, 128),
        dma(8), dma(4), dma(4), dma(NPX), dma(NPX), dma(NPX), dma(NPX), dma(NPX), dma(NPX),
        dma(NPZ), dma(NPY), dma(NPZ), dma(NPY), dma(NPY), dma(NPZ),
    ]
    result = pl.pallas_call(
        kernel,
        out_shape=jax.ShapeDtypeStruct((V, ROWS, 128), F32),
        in_specs=[pl.BlockSpec(memory_space=pltpu.HBM)] * 8,
        out_specs=pl.BlockSpec(memory_space=pltpu.VMEM),
        scratch_shapes=scratch,
        compiler_params=pltpu.CompilerParams(collective_id=0, has_side_effects=True),
        name="adi",
    )(*args)
    return result.reshape(shape)


def solution(mesh):
    vector, matrix = P(None, "px", "py", None), P(None, None, "px", "py", None)
    return jax.shard_map(
        per_device, mesh=mesh, in_specs=(vector,) * 2 + (matrix,) * 6, out_specs=vector, check_vma=False
    )
```

```python
import jax
import jax.numpy as jnp
from jax import lax
from jax.experimental import pallas as pl
from jax.experimental.pallas import tpu as pltpu
from jax.sharding import PartitionSpec as P

DISSIPATION = 0.1
MESH = pl.DeviceIdType.MESH
F32 = jnp.float32

V = 5
E = V * V
NPX, NPY, NPZ = 8, 32, 8
IN_Z = NPY // NPZ
CX, CY = 8, 16
ROWS = CX * CY
XM, YM = 76, 80
XV, YV = 12, 16
YMP, YVP, YP = 88, 24, 24
CHIPS = NPX // 2
XO = CY // NPX


def block(ref, rows):
    return ref[:, rows, :].reshape(V, V, 8, 128)


def total(terms):
    while len(terms) > 1:
        terms = [terms[k] + terms[k + 1] if k + 1 < len(terms) else terms[k] for k in range(0, len(terms), 2)]
    return terms[0]


def apply(m, x):
    return total([m[:, c] * x[c][None] for c in range(V)])


def product(m, b):
    rows = [total([m[a, c][None] * b[c] for c in range(V)]) for a in range(V)]
    return jnp.stack(rows)


def device_products(lo, up, up_again, n, psi, emit, before_up=lambda: None):
    first = lo(0)
    psi[0] = first

    def forward(i, m):
        m = product(lo(i), m)
        psi[i] = m
        return m

    last = lax.fori_loop(1, n, forward, first)
    emit(0, last)
    before_up()

    def backward(t, z):
        i = n - 2 - t
        return psi[i] + product(up(i), z)

    emit(E, lax.fori_loop(0, n - 1, backward, last))

    def upward(t, m):
        return product(up_again(n - 2 - t), m)

    emit(2 * E, lax.fori_loop(0, n - 1, upward, up(n - 1)))


def forward_cells(source, lo, n, start, save):
    def step(i, carry):
        out = []
        for t, f in enumerate(carry):
            cur = source(i, t)
            if f is not None:
                cur = cur - apply(lo(i, t), f)
            save(i, t, cur)
            out.append(cur)
        return tuple(out)

    begin = 0
    if start[0] is None:
        start, begin = step(0, start), 1
    return lax.fori_loop(begin, n, step, start)


def backward_cells(source, up, n, start, save):
    def step(k, carry):
        i = n - 1 - k
        out = []
        for t, g in enumerate(carry):
            cur = source(i, t)
            if g is not None:
                cur = cur - apply(up(i, t), g)
            if save is not None:
                save(i, t, cur)
            out.append(cur)
        return tuple(out)

    begin = 0
    if start[0] is None:
        start, begin = step(0, start), 1
    return lax.fori_loop(begin, n, step, start)


def kernel(field, forcing, xi, xl, xu, yi, yl, yu, out,
           fx, fo, xi_v, xl_v, xu_v, yi_v, yl_v, yu_v, yi_t, yl_t, yu_t,
           fy, hx, hy, rhs, psi, sx, fwx, sy, fwy,
           pm, pv, xm_out, xm_in, xv_out, xv_in, xr_out, xr_in,
           ym_out, ym_in, yv_out, yv_in, yr_out, yr_in, xmat, ymat, cmat,
           load_s, halo_ss, halo_rs, pair_ss, pair_rs, xm_ss, xm_rs, xv_ss, xv_rs, xr_ss, xr_rs,
           ym_ss, ym_rs, yv_ss, yv_rs, yr_ss, yr_rs):
    px, py = lax.axis_index("px"), lax.axis_index("py")
    core, chip, z = lax.rem(px, 2), lax.div(px, 2), lax.div(py, IN_Z)
    partner = px + 1 - 2 * core

    def owner_of(r):
        return IN_Z * r + lax.rem(2 * core + r, IN_Z)

    is_owner = py == owner_of(z)

    mine = slice(2 * CY, 2 * CY + ROWS)

    def load(k, src, dst):
        return pltpu.make_async_copy(src, dst, load_s.at[k])

    padded = (slice(None), slice(None), slice(0, CY))
    in_xl, in_xu, in_field = load(0, xl, xl_v), load(1, xu, xu_v), load(2, field, fx.at[:, mine, :])
    in_yl, in_yu, in_yi = load(3, yl, yl_v.at[padded]), load(4, yu, yu_v.at[padded]), load(5, yi, yi_v.at[padded])
    in_fo, in_xi = load(6, forcing, fo), load(7, xi, xi_v)
    for c in (in_xl, in_xu, in_field):
        c.start()

    barrier = pltpu.get_barrier_semaphore()

    def greet_x(k, _):
        pl.semaphore_signal(barrier, inc=1, device_id=(lax.rem(px + k, NPX), py), device_id_type=MESH)
        return 0

    def greet_y(k, _):
        pl.semaphore_signal(barrier, inc=1, device_id=(px, lax.rem(py + k, NPY)), device_id_type=MESH)
        return 0

    lax.fori_loop(1, NPX, greet_x, 0)
    lax.fori_loop(1, NPY, greet_y, 0)

    def x_rows(i, h):
        return pl.ds(pl.multiple_of(CY * i + 8 * h, 8), 8)

    def y_rows(j):
        return pl.ds(j, 8, stride=CY)

    def turned(ref, j):
        return ref.reshape(E, CX * YP, 128)[:, pl.ds(j, 8, stride=YP), :].reshape(V, V, 8, 128)

    def x_block(ref):
        return lambda i, h: block(ref, x_rows(i, h))

    def y_block(ref):
        return lambda j, _=0: ref[j]

    def at(ref, k, size, pitch=None):
        return ref.at[pl.ds(pl.multiple_of(k * (pitch or size), 8), size), :]

    def x_copy(src, dst, ss, rs, size, c):
        return pltpu.make_async_remote_copy(
            at(src, c, size), at(dst, chip, size), ss.at[c], rs.at[chip],
            device_id=(2 * c + core, py), device_id_type=MESH)

    def other_chip(k):
        return lax.rem(chip + k, CHIPS)

    def x_send(src, dst, ss, rs, size):
        for k in range(1, CHIPS):
            x_copy(src, dst, ss, rs, size, other_chip(k)).start()
        pltpu.make_async_copy(at(src, chip, size), at(dst, chip, size), rs.at[chip]).start()

    def x_sent(src, dst, ss, rs, size):
        for k in range(1, CHIPS):
            x_copy(src, dst, ss, rs, size, other_chip(k)).wait_send()

    def x_back(k):
        d = lax.rem(px + k, NPX)
        return pltpu.make_async_remote_copy(
            at(xr_out, lax.div(d, 2), XO * XV), at(xr_in, CHIPS * core + chip, XO * XV), xr_ss.at[d],
            xr_rs.at[CHIPS * core + chip], device_id=(d, py), device_id_type=MESH)

    def pair_copy(k, ref):
        return pltpu.make_async_remote_copy(
            ref, ref, pair_ss.at[k], pair_rs.at[k], device_id=(partner, py), device_id_type=MESH)

    pairs = [pair_copy(0, pm.at[core, 1 - core]), pair_copy(1, pm.at[core, core]), pair_copy(2, pv.at[core])]

    def received(dst, rs, size, count, pitch=None):
        def one(k, _):
            pltpu.make_async_copy(at(dst, k, size, pitch), at(dst, k, size, pitch), rs.at[k]).wait()
            return 0

        lax.fori_loop(0, count, one, 0)

    def slot(d):
        return NPZ * lax.rem(d, IN_Z) + lax.div(d, IN_Z)

    def y_copy(src, dst, ss, rs, size, pitch, r):
        return pltpu.make_async_remote_copy(
            at(src, r, size, pitch), at(dst, slot(py), size, pitch), ss.at[r], rs.at[slot(py)],
            device_id=(px, owner_of(r)), device_id_type=MESH)

    def y_send(src, dst, ss, rs, size, pitch):
        @pl.when(is_owner)
        def _():
            pltpu.make_async_copy(at(src, z, size, pitch), at(dst, slot(py), size, pitch), rs.at[slot(py)]).start()

        @pl.when(jnp.logical_not(is_owner))
        def _():
            y_copy(src, dst, ss, rs, size, pitch, z).start()

        def one(k, _):
            y_copy(src, dst, ss, rs, size, pitch, lax.rem(z + k, NPZ)).start()
            return 0

        lax.fori_loop(1, NPZ, one, 0)

    def y_sent(src, dst, ss, rs, size, pitch):
        @pl.when(jnp.logical_not(is_owner))
        def _():
            y_copy(src, dst, ss, rs, size, pitch, z).wait_send()

        def one(k, _):
            y_copy(src, dst, ss, rs, size, pitch, lax.rem(z + k, NPZ)).wait_send()
            return 0

        lax.fori_loop(1, NPZ, one, 0)

    xm = (xm_out, xm_in, xm_ss, xm_rs, XO * XM)
    xv = (xv_out, xv_in, xv_ss, xv_rs, XO * XV)
    ym = (ym_out, ym_in, ym_ss, ym_rs, YM, YMP)
    yv = (yv_out, yv_in, yv_ss, yv_rs, YV, YVP)
    in_field.wait()

    def turn(j, _):
        fy[2 + j] = fx[:, pl.ds(2 * CY + j, 8, stride=CY), :]
        return 0

    lax.fori_loop(0, CY, turn, 0)

    right, left = lax.rem(px + 1, NPX), lax.rem(px + NPX - 1, NPX)
    north, south = lax.rem(py + 1, NPY), lax.rem(py + NPY - 1, NPY)
    halos = [
        pltpu.make_async_remote_copy(a, b, halo_ss.at[k], halo_rs.at[k], device_id=d, device_id_type=MESH)
        for k, (a, b, d) in enumerate([
            (fx.at[:, ROWS : ROWS + 2 * CY, :], hx.at[0], (right, py)),
            (fx.at[:, 2 * CY : 4 * CY, :], hx.at[1], (left, py)),
            (fy.at[CY : CY + 2], hy.at[0], (px, north)),
            (fy.at[2:4], hy.at[1], (px, south))])
    ]
    in_xl.wait()
    in_yl.start()
    in_yu.start()
    for first, h in ((True, 1 - core), (False, core)):
        def emit(base, m, h=h):
            pm[core, h, pl.ds(base, E)] = m.reshape(E, 8, 128)

        def before_up(first=first):
            if first:
                in_xu.wait()
                for c in (in_fo, in_xi, in_yi):
                    c.start()

        lo, up = [lambda i, ref=ref, h=h: block(ref, x_rows(i, h)) for ref in (xl_v, xu_v)]
        device_products(lo, up, up, CX, psi, emit, before_up)
        if first:
            pl.semaphore_wait(barrier, NPX + NPY - 2)
            pairs[0].start()
            for c in halos:
                c.start()
        else:
            pairs[1].start()

    pairs[0].wait()

    def half(d, k):
        return pm[d, core, pl.ds(k * E, E)].reshape(V, V, 8, 128)

    def emit_x(base, m):
        for e in range(E):
            xm_out[pl.ds(base + e, 8, stride=XM), :] = m[e // V, e % V]

    m0, n0 = half(0, 0), half(0, 2)
    emit_x(0, product(half(1, 0), m0))
    emit_x(E, half(0, 1) + product(n0, product(half(1, 1), m0)))
    emit_x(2 * E, product(n0, half(1, 2)))
    x_send(*xm)

    in_fo.wait()
    for c in halos:
        c.wait()
    fx[:, 0 : 2 * CY, :] = jnp.where(px == 0, 0.0, hx[0])
    fx[:, 2 * CY + ROWS :, :] = jnp.where(px == NPX - 1, 0.0, hx[1])
    fy[0:2] = jnp.where(py == 0, 0.0, hy[0])
    fy[CY + 2 :] = jnp.where(py == NPY - 1, 0.0, hy[1])

    def difference(v):
        return v[0] - 4.0 * v[1] + 6.0 * v[2] - 4.0 * v[3] + v[4]

    def along_y(j, _):
        d = difference([fy[j + k] for k in range(5)])
        rhs[:, y_rows(j), :] = fo[:, y_rows(j), :] - DISSIPATION * d
        return 0

    lax.fori_loop(0, CY, along_y, 0)
    in_xi.wait()

    def x_source(i, h):
        d = difference([fx[:, x_rows(i + k, h), :] for k in range(5)])
        s = apply(block(xi_v, x_rows(i, h)), rhs[:, x_rows(i, h), :] - DISSIPATION * d)
        sx[:, x_rows(i, h), :] = s
        return s

    def save_fwx(i, h, f):
        fwx[:, x_rows(i, h), :] = f

    def load_fwx(i, h):
        return fwx[:, x_rows(i, h), :]

    ends = forward_cells(x_source, x_block(xl_v), CX, (None, None), save_fwx)
    starts = backward_cells(load_fwx, x_block(xu_v), CX, (None, None), None)
    for h in range(2):
        pv[core, h, pl.ds(0, V)] = ends[h]
        pv[core, h, pl.ds(V, V)] = starts[h]
    pairs[2].start()

    in_yl.wait()

    def emit_y(base, m):
        for e in range(E):
            ym_out[pl.ds(base + e, 8, stride=YMP), :] = m[e // V, e % V]

    def lo_y(j):
        m = turned(yl_v, j)
        yl_t[j] = m
        return m

    def up_y(j):
        m = turned(yu_v, j)
        yu_t[j] = m
        return m

    device_products(lo_y, up_y, y_block(yu_t), CY, psi, emit_y, in_yu.wait)
    y_send(*ym)

    pairs[2].wait()

    def part(d, h, k):
        return pv[d, h, pl.ds(k * V, V)]

    v0 = part(0, core, 0)
    v = part(1, core, 0) + apply(half(1, 0), v0)
    w = part(0, core, 1) + apply(half(0, 2), part(1, core, 1) - apply(half(1, 1), v0))
    for c in range(V):
        xv_out[pl.ds(c, 8, stride=XV), :] = v[c]
        xv_out[pl.ds(V + c, 8, stride=XV), :] = w[c]
    x_send(*xv)

    place = lax.broadcasted_iota(jnp.int32, (V, 8, 128), 1)

    def chain(m, v, by, count):
        def one(_, a):
            return tuple(jnp.where(place < by, 0.0, pltpu.roll(vk + apply(mk(), ak), by, axis=1))
                         for vk, mk, ak in zip(v, m, a))

        return lax.fori_loop(0, count, one, tuple(jnp.zeros((V, 8, 128), F32) for _ in v))

    def chain_back(m, v, by, count):
        def one(_, b):
            return tuple(jnp.where(place >= 8 - by, 0.0, pltpu.roll(vk + apply(mk(), bk), 8 - by, axis=1))
                         for vk, mk, bk in zip(v, m, b))

        return lax.fori_loop(0, count, one, tuple(jnp.zeros((V, 8, 128), F32) for _ in v))

    def held(ref, *at_):
        return lambda: ref[at_].reshape(V, V, 8, 128)

    in_yi.wait()

    def turn_yi(j, _):
        yi_t[j] = turned(yi_v, j)
        return 0

    lax.fori_loop(0, CY, turn_yi, 0)

    received(xm_in, xm_rs, XO * XM, CHIPS)
    for e in range(3 * E):
        xmat[e // E, e % E] = xm_in[pl.ds(e, 8, stride=XM), :]
    received(xv_in, xv_rs, XO * XV, CHIPS)

    def rows_of(ref, first, stride):
        return jnp.stack([ref[pl.ds(first + c, 8, stride=stride), :] for c in range(V)])

    a, = chain([held(xmat, 0)], [rows_of(xv_in, 0, XV)], XO, CHIPS - 1)
    b, = chain_back([held(xmat, 2)], [rows_of(xv_in, V, XV) - apply(held(xmat, 1)(), a)], XO, CHIPS - 1)
    for c in range(V):
        xr_out[pl.ds(c, 8, stride=XV), :] = a[c]
        xr_out[pl.ds(V + c, 8, stride=XV), :] = b[c]
    own = CHIPS * core + chip
    pltpu.make_async_copy(at(xr_out, chip, XO * XV), at(xr_in, own, XO * XV), xr_rs.at[own]).start()
    for k in range(1, NPX):
        x_back(k).start()
    pairs[1].wait()
    received(xr_in, xr_rs, XO * XV, NPX)

    before, after = [], []
    for h in range(2):
        a, b = rows_of(xr_in, 8 * h * XV, XV), rows_of(xr_in, 8 * h * XV + V, XV)

        def of(d, k, h=h):
            return pm[d, h, pl.ds(k * E, E)].reshape(V, V, 8, 128)

        a1 = part(0, h, 0) + apply(of(0, 0), a)
        b0 = part(1, h, 1) - apply(of(1, 1), a1) + apply(of(1, 2), b)
        before.append(jnp.where(core == 0, a, a1))
        after.append(jnp.where(core == 0, b0, b))

    def load_sx(i, h):
        return sx[:, x_rows(i, h), :]

    forward_cells(load_sx, x_block(xl_v), CX, tuple(before), save_fwx)
    backward_cells(load_fwx, x_block(xu_v), CX, tuple(after), save_fwx)

    def y_source(j, _):
        s = apply(yi_t[j], fwx[:, y_rows(j), :])
        sy[j] = s
        return s

    def save_fwy(j, _, f):
        fwy[j] = f

    def load_fwy(j, _):
        return fwy[j]

    end, = forward_cells(y_source, y_block(yl_t), CY, (None,), save_fwy)
    start, = backward_cells(load_fwy, y_block(yu_t), CY, (None,), None)
    for c in range(V):
        yv_out[pl.ds(c, 8, stride=YVP), :] = end[c]
        yv_out[pl.ds(V + c, 8, stride=YVP), :] = start[c]
    y_send(*yv)

    def y_back(d):
        return pltpu.make_async_remote_copy(
            at(yr_out, slot(d), YV, YVP), at(yr_in, z, YV, YVP), yr_ss.at[d], yr_rs.at[z], device_id=(px, d), device_id_type=MESH)

    @pl.when(is_owner)
    def _():
        received(ym_in, ym_rs, YM, NPY, YMP)
        for d in range(IN_Z):
            for e in range(3 * E):
                ymat[d, e // E, e % E] = ym_in[pl.ds(d * NPZ * YMP + e, 8, stride=YMP), :]
        mm, mz, mn = [[held(ymat, d, k) for d in range(IN_Z)] for k in range(3)]

        def keep(k, m):
            cmat[k] = m.reshape(E, 8, 128)

        phi = mm[0]()
        x = []
        for d in range(1, IN_Z):
            keep(3 + d, product(mz[d](), phi))
            phi = product(mm[d](), phi)
        keep(0, phi)
        x = held(cmat, 3 + IN_Z - 1)()
        for d in range(IN_Z - 2, 0, -1):
            x = held(cmat, 3 + d)() + product(mn[d](), x)
        keep(1, mz[0]() + product(mn[0](), x))
        n = mn[IN_Z - 1]()
        for d in range(IN_Z - 2, -1, -1):
            n = product(mn[d](), n)
        keep(2, n)

        received(yv_in, yv_rs, YV, NPY, YVP)
        v = [rows_of(yv_in, d * NPZ * YVP, YVP) for d in range(IN_Z)]
        w = [rows_of(yv_in, d * NPZ * YVP + V, YVP) for d in range(IN_Z)]
        e = v[0]
        ins = [None]
        for d in range(1, IN_Z):
            ins.append(e)
            e = v[d] + apply(mm[d](), e)
        g = w[IN_Z - 1] - apply(mz[IN_Z - 1](), ins[IN_Z - 1])
        for d in range(IN_Z - 2, -1, -1):
            g = w[d] + apply(mn[d](), g)
            if d:
                g = g - apply(mz[d](), ins[d])
        a, = chain([held(cmat, 0)], [e], 1, NPZ - 1)
        g = g - apply(held(cmat, 1)(), a)
        b, = chain_back([held(cmat, 2)], [g], 1, NPZ - 1)
        ins = [a]
        for d in range(IN_Z - 1):
            ins.append(v[d] + apply(mm[d](), ins[d]))
        ahead = [None] * IN_Z
        ahead[IN_Z - 1] = b
        for d in range(IN_Z - 1, 0, -1):
            ahead[d - 1] = w[d] - apply(mz[d](), ins[d]) + apply(mn[d](), ahead[d])
        for d in range(IN_Z):
            for c in range(V):
                yr_out[pl.ds(d * NPZ * YVP + c, 8, stride=YVP), :] = ins[d][c]
                yr_out[pl.ds(d * NPZ * YVP + V + c, 8, stride=YVP), :] = ahead[d][c]

        pltpu.make_async_copy(at(yr_out, slot(py), YV, YVP), at(yr_in, z, YV, YVP), yr_rs.at[z]).start()

        def one(k, _):
            y_back(lax.rem(py + k, NPY)).start()
            return 0

        lax.fori_loop(1, NPY, one, 0)

    received(yr_in, yr_rs, YV, NPZ, YVP)

    def load_sy(j, _):
        return sy[j]

    def save_res(j, _, u):
        out[:, y_rows(j), :] = u

    forward_cells(load_sy, y_block(yl_t), CY, (rows_of(yr_in, 0, YVP),), save_fwy)
    backward_cells(load_fwy, y_block(yu_t), CY, (rows_of(yr_in, V, YVP),), save_res)

    x_sent(*xm)
    x_sent(*xv)
    for k in range(1, NPX):
        x_back(k).wait_send()
    y_sent(*ym)
    y_sent(*yv)

    @pl.when(is_owner)
    def _():
        def one(k, _):
            y_back(lax.rem(py + k, NPY)).wait_send()
            return 0

        lax.fori_loop(1, NPY, one, 0)


def per_device(field, forcing, *blocks):
    shape = field.shape
    args = [v.reshape(V, ROWS, 128) for v in (field, forcing)] + [m.reshape(E, ROWS, 128) for m in blocks[:3]]
    args += [m.reshape(E, CX, CY, 128) for m in blocks[3:]]

    def vmem(*dims):
        return pltpu.VMEM(dims, F32)

    def dma(n):
        return pltpu.SemaphoreType.DMA((n,))

    scratch = [
        vmem(V, ROWS + 4 * CY, 128), vmem(V, ROWS, 128), *[vmem(E, ROWS, 128) for _ in range(3)],
        *[vmem(E, CX, YP, 128) for _ in range(3)], *[vmem(CY, V, V, 8, 128) for _ in range(3)],
        vmem(CY + 4, V, 8, 128), vmem(2, V, 2 * CY, 128), vmem(2, 2, V, 8, 128), vmem(V, ROWS, 128),
        vmem(CY, V, V, 8, 128), vmem(V, ROWS, 128), vmem(V, ROWS, 128), vmem(CY, V, 8, 128), vmem(CY, V, 8, 128),
        vmem(2, 2, 3 * E, 8, 128), vmem(2, 2, 2 * V, 8, 128), vmem(8 * XM, 128), vmem(8 * XM, 128),
        vmem(8 * XV, 128), vmem(8 * XV, 128), vmem(8 * XV, 128), vmem(CY * XV, 128),
        vmem(CX * YMP, 128), vmem(NPY * YMP, 128),
        vmem(CX * YVP, 128), vmem(NPY * YVP, 128), vmem(NPY * YVP, 128), vmem(CX * YVP, 128),
        vmem(3, E, 8, 128), vmem(IN_Z, 3, E, 8, 128), vmem(3 + IN_Z, E, 8, 128),
        dma(8), dma(4), dma(4), dma(3), dma(3), dma(CHIPS), dma(CHIPS), dma(CHIPS), dma(CHIPS), dma(NPX), dma(NPX),
        dma(NPZ), dma(NPY), dma(NPZ), dma(NPY), dma(NPY), dma(NPZ),
    ]
    result = pl.pallas_call(
        kernel,
        out_shape=jax.ShapeDtypeStruct((V, ROWS, 128), F32),
        in_specs=[pl.BlockSpec(memory_space=pltpu.HBM)] * 8,
        out_specs=pl.BlockSpec(memory_space=pltpu.VMEM),
        scratch_shapes=scratch,
        compiler_params=pltpu.CompilerParams(collective_id=0, has_side_effects=True, vmem_limit_bytes=56000000),
        name="adi",
    )(*args)
    return result.reshape(shape)


def solution(mesh):
    vector, matrix = P(None, "px", "py", None), P(None, None, "px", "py", None)
    return jax.shard_map(
        per_device, mesh=mesh, in_specs=(vector,) * 2 + (matrix,) * 6, out_specs=vector, check_vma=False
    )
```

```python
import jax
import jax.numpy as jnp
from jax import lax
from jax.experimental import pallas as pl
from jax.experimental.pallas import tpu as pltpu
from jax.sharding import PartitionSpec as P

DISSIPATION = 0.1
MESH = pl.DeviceIdType.MESH
F32 = jnp.float32

V = 5
E = V * V
NPX, NPY, NPZ = 8, 32, 8
IN_Z = NPY // NPZ
CX, CY = 8, 16
ROWS = CX * CY
XM, YM = 76, 75
XV, YV = 12, 10
YMP, YVP, YP = 88, 24, 24
CHIPS = NPX // 2
XO = CY // NPX


def block(ref, rows):
    return ref[:, rows, :].reshape(V, V, 8, 128)


def total(terms):
    while len(terms) > 1:
        terms = [terms[k] + terms[k + 1] if k + 1 < len(terms) else terms[k] for k in range(0, len(terms), 2)]
    return terms[0]


def apply(m, x):
    return total([m[:, c] * x[c][None] for c in range(V)])


def product(m, b):
    rows = [total([m[a, c][None] * b[c] for c in range(V)]) for a in range(V)]
    return jnp.stack(rows)


def device_products(lo, up, up_again, n, psi, emit, before_up=lambda: None):
    first = lo(0)
    psi[0] = first

    def forward(i, m):
        m = product(lo(i), m)
        psi[i] = m
        return m

    last = lax.fori_loop(1, n, forward, first)
    emit(0, last)
    before_up()

    def backward(t, z):
        i = n - 2 - t
        return psi[i] + product(up(i), z)

    emit(E, lax.fori_loop(0, n - 1, backward, last))

    def upward(t, m):
        return product(up_again(n - 2 - t), m)

    emit(2 * E, lax.fori_loop(0, n - 1, upward, up(n - 1)))


def forward_cells(source, lo, n, start, save):
    def step(i, carry):
        out = []
        for t, f in enumerate(carry):
            cur = source(i, t)
            if f is not None:
                cur = cur - apply(lo(i, t), f)
            save(i, t, cur)
            out.append(cur)
        return tuple(out)

    begin = 0
    if start[0] is None:
        start, begin = step(0, start), 1
    return lax.fori_loop(begin, n, step, start)


def backward_cells(source, up, n, start, save):
    def step(k, carry):
        i = n - 1 - k
        out = []
        for t, g in enumerate(carry):
            cur = source(i, t)
            if g is not None:
                cur = cur - apply(up(i, t), g)
            if save is not None:
                save(i, t, cur)
            out.append(cur)
        return tuple(out)

    begin = 0
    if start[0] is None:
        start, begin = step(0, start), 1
    return lax.fori_loop(begin, n, step, start)


def kernel(field, forcing, xi, xl, xu, yi, yl, yu, out,
           fx, fo, xi_v, xl_v, xu_v, yi_v, yl_v, yu_v, yi_t, yl_t, yu_t,
           fy, hx, hy, rhs, psi, sx, fwx, sy, fwy,
           pm, pv, xm_out, xm_in, xv_out, xv_in, xr_out, xr_in,
           ym_out, ym_in, yv_out, yv_in, yr_out, yr_in, xmat, ymat, cmat,
           load_s, halo_ss, halo_rs, pair_ss, pair_rs, xm_ss, xm_rs, xv_ss, xv_rs, xr_ss, xr_rs,
           ym_ss, ym_rs, yv_ss, yv_rs, yr_ss, yr_rs):
    px, py = lax.axis_index("px"), lax.axis_index("py")
    core, chip, z = lax.rem(px, 2), lax.div(px, 2), lax.div(py, IN_Z)
    partner = px + 1 - 2 * core

    def owner_of(r):
        return IN_Z * r + lax.rem(2 * core + r, IN_Z)

    is_owner = py == owner_of(z)

    mine = slice(2 * CY, 2 * CY + ROWS)

    def load(k, src, dst):
        return pltpu.make_async_copy(src, dst, load_s.at[k])

    padded = (slice(None), slice(None), slice(0, CY))
    in_xl, in_xu, in_field = load(0, xl, xl_v), load(1, xu, xu_v), load(2, field, fx.at[:, mine, :])
    in_yl, in_yu, in_yi = load(3, yl, yl_v.at[padded]), load(4, yu, yu_v.at[padded]), load(5, yi, yi_v.at[padded])
    in_fo, in_xi = load(6, forcing, fo), load(7, xi, xi_v)
    for c in (in_xl, in_xu, in_field):
        c.start()

    barrier = pltpu.get_barrier_semaphore()

    def greet_x(k, _):
        pl.semaphore_signal(barrier, inc=1, device_id=(lax.rem(px + k, NPX), py), device_id_type=MESH)
        return 0

    def greet_y(k, _):
        pl.semaphore_signal(barrier, inc=1, device_id=(px, lax.rem(py + k, NPY)), device_id_type=MESH)
        return 0

    lax.fori_loop(1, NPX, greet_x, 0)
    lax.fori_loop(1, NPY, greet_y, 0)

    def x_rows(i, h):
        return pl.ds(pl.multiple_of(CY * i + 8 * h, 8), 8)

    def y_rows(j):
        return pl.ds(j, 8, stride=CY)

    def turned(ref, j):
        return ref.reshape(E, CX * YP, 128)[:, pl.ds(j, 8, stride=YP), :].reshape(V, V, 8, 128)

    def x_block(ref):
        return lambda i, h: block(ref, x_rows(i, h))

    def y_block(ref):
        return lambda j, _=0: ref[j]

    def at(ref, k, size, pitch=None):
        return ref.at[pl.ds(pl.multiple_of(k * (pitch or size), 8), size), :]

    def x_copy(src, dst, ss, rs, size, c):
        return pltpu.make_async_remote_copy(
            at(src, c, size), at(dst, chip, size), ss.at[c], rs.at[chip],
            device_id=(2 * c + core, py), device_id_type=MESH)

    def other_chip(k):
        return lax.rem(chip + k, CHIPS)

    def x_send(src, dst, ss, rs, size):
        for k in (2, 1, 3):
            x_copy(src, dst, ss, rs, size, other_chip(k)).start()
        pltpu.make_async_copy(at(src, chip, size), at(dst, chip, size), rs.at[chip]).start()

    def x_sent(src, dst, ss, rs, size):
        for k in range(1, CHIPS):
            x_copy(src, dst, ss, rs, size, other_chip(k)).wait_send()

    def x_back(k):
        d = 2 * other_chip(k // 2) + lax.rem(core + k, 2)
        return pltpu.make_async_remote_copy(
            at(xr_out, lax.div(d, 2), XO * XV), at(xr_in, CHIPS * core + chip, XO * XV), xr_ss.at[d],
            xr_rs.at[CHIPS * core + chip], device_id=(d, py), device_id_type=MESH)

    def pair_copy(k, ref):
        return pltpu.make_async_remote_copy(
            ref, ref, pair_ss.at[k], pair_rs.at[k], device_id=(partner, py), device_id_type=MESH)

    pairs = [pair_copy(0, pm.at[core, 1 - core]), pair_copy(1, pm.at[core, core]), pair_copy(2, pv.at[core])]

    def received(dst, rs, size, count, pitch=None):
        def one(k, _):
            pltpu.make_async_copy(at(dst, k, size, pitch), at(dst, k, size, pitch), rs.at[k]).wait()
            return 0

        lax.fori_loop(0, count, one, 0)

    def slot(d):
        return NPZ * lax.rem(d, IN_Z) + lax.div(d, IN_Z)

    def y_copy(src, dst, ss, rs, size, pitch, r):
        return pltpu.make_async_remote_copy(
            at(src, r, size, pitch), at(dst, slot(py), size, pitch), ss.at[r], rs.at[slot(py)],
            device_id=(px, owner_of(r)), device_id_type=MESH)

    def y_send(src, dst, ss, rs, size, pitch):
        for k in (4, 3, 5, 2, 6, 1, 7):
            y_copy(src, dst, ss, rs, size, pitch, lax.rem(z + k, NPZ)).start()

        @pl.when(is_owner)
        def _():
            pltpu.make_async_copy(at(src, z, size, pitch), at(dst, slot(py), size, pitch), rs.at[slot(py)]).start()

        @pl.when(jnp.logical_not(is_owner))
        def _():
            y_copy(src, dst, ss, rs, size, pitch, z).start()

    def y_sent(src, dst, ss, rs, size, pitch):
        @pl.when(jnp.logical_not(is_owner))
        def _():
            y_copy(src, dst, ss, rs, size, pitch, z).wait_send()

        def one(k, _):
            y_copy(src, dst, ss, rs, size, pitch, lax.rem(z + k, NPZ)).wait_send()
            return 0

        lax.fori_loop(1, NPZ, one, 0)

    xm = (xm_out, xm_in, xm_ss, xm_rs, XO * XM)
    xv = (xv_out, xv_in, xv_ss, xv_rs, XO * XV)
    ym = (ym_out, ym_in, ym_ss, ym_rs, YM, YMP)
    yv = (yv_out, yv_in, yv_ss, yv_rs, YV, YVP)
    in_field.wait()

    def turn(j, _):
        fy[2 + j] = fx[:, pl.ds(2 * CY + j, 8, stride=CY), :]
        return 0

    lax.fori_loop(0, CY, turn, 0)

    right, left = lax.rem(px + 1, NPX), lax.rem(px + NPX - 1, NPX)
    north, south = lax.rem(py + 1, NPY), lax.rem(py + NPY - 1, NPY)
    halos = [
        pltpu.make_async_remote_copy(a, b, halo_ss.at[k], halo_rs.at[k], device_id=d, device_id_type=MESH)
        for k, (a, b, d) in enumerate([
            (fx.at[:, ROWS : ROWS + 2 * CY, :], hx.at[0], (right, py)),
            (fx.at[:, 2 * CY : 4 * CY, :], hx.at[1], (left, py)),
            (fy.at[CY : CY + 2], hy.at[0], (px, north)),
            (fy.at[2:4], hy.at[1], (px, south))])
    ]
    in_xl.wait()
    in_yl.start()
    in_yu.start()
    for first, h in ((True, 1 - core), (False, core)):
        def emit(base, m, h=h):
            pm[core, h, pl.ds(base, E)] = m.reshape(E, 8, 128)

        def before_up(first=first):
            if first:
                in_xu.wait()
                for c in (in_fo, in_xi, in_yi):
                    c.start()

        lo, up = [lambda i, ref=ref, h=h: block(ref, x_rows(i, h)) for ref in (xl_v, xu_v)]
        device_products(lo, up, up, CX, psi, emit, before_up)
        if first:
            pl.semaphore_wait(barrier, NPX + NPY - 2)
            pairs[0].start()
            for c in halos:
                c.start()
        else:
            pairs[1].start()

    in_yl.wait()

    def emit_y(base, m):
        for e in range(E):
            ym_out[pl.ds(base + e, 8, stride=YMP), :] = m[e // V, e % V]

    def lo_y(j):
        m = turned(yl_v, j)
        yl_t[j] = m
        return m

    def up_y(j):
        m = turned(yu_v, j)
        yu_t[j] = m
        return m

    device_products(lo_y, up_y, y_block(yu_t), CY, psi, emit_y, in_yu.wait)
    y_send(*ym)

    pairs[0].wait()

    def half(d, k):
        return pm[d, core, pl.ds(k * E, E)].reshape(V, V, 8, 128)

    def emit_x(base, m):
        for e in range(E):
            xm_out[pl.ds(base + e, 8, stride=XM), :] = m[e // V, e % V]

    m0, n0 = half(0, 0), half(0, 2)
    emit_x(0, product(half(1, 0), m0))
    emit_x(E, half(0, 1) + product(n0, product(half(1, 1), m0)))
    emit_x(2 * E, product(n0, half(1, 2)))
    x_send(*xm)

    in_fo.wait()
    for c in halos:
        c.wait()
    fx[:, 0 : 2 * CY, :] = jnp.where(px == 0, 0.0, hx[0])
    fx[:, 2 * CY + ROWS :, :] = jnp.where(px == NPX - 1, 0.0, hx[1])
    fy[0:2] = jnp.where(py == 0, 0.0, hy[0])
    fy[CY + 2 :] = jnp.where(py == NPY - 1, 0.0, hy[1])

    def difference(v):
        return v[0] - 4.0 * v[1] + 6.0 * v[2] - 4.0 * v[3] + v[4]

    def along_y(j, _):
        d = difference([fy[j + k] for k in range(5)])
        rhs[:, y_rows(j), :] = fo[:, y_rows(j), :] - DISSIPATION * d
        return 0

    lax.fori_loop(0, CY, along_y, 0)
    in_xi.wait()

    def x_source(i, h):
        d = difference([fx[:, x_rows(i + k, h), :] for k in range(5)])
        s = apply(block(xi_v, x_rows(i, h)), rhs[:, x_rows(i, h), :] - DISSIPATION * d)
        sx[:, x_rows(i, h), :] = s
        return s

    def save_fwx(i, h, f):
        fwx[:, x_rows(i, h), :] = f

    def load_fwx(i, h):
        return fwx[:, x_rows(i, h), :]

    ends = forward_cells(x_source, x_block(xl_v), CX, (None, None), save_fwx)
    starts = backward_cells(load_fwx, x_block(xu_v), CX, (None, None), None)
    for h in range(2):
        pv[core, h, pl.ds(0, V)] = ends[h]
        pv[core, h, pl.ds(V, V)] = starts[h]
    pairs[2].start()

    pairs[2].wait()

    def part(d, h, k):
        return pv[d, h, pl.ds(k * V, V)]

    v0 = part(0, core, 0)
    v = part(1, core, 0) + apply(half(1, 0), v0)
    w = part(0, core, 1) + apply(half(0, 2), part(1, core, 1) - apply(half(1, 1), v0))
    for c in range(V):
        xv_out[pl.ds(c, 8, stride=XV), :] = v[c]
        xv_out[pl.ds(V + c, 8, stride=XV), :] = w[c]
    x_send(*xv)

    place = lax.broadcasted_iota(jnp.int32, (V, 8, 128), 1)

    def chain(m, v, by, count):
        def one(_, a):
            return tuple(jnp.where(place < by, 0.0, pltpu.roll(vk + apply(mk(), ak), by, axis=1))
                         for vk, mk, ak in zip(v, m, a))

        return lax.fori_loop(0, count, one, tuple(jnp.zeros((V, 8, 128), F32) for _ in v))

    def chain_back(m, v, by, count):
        def one(_, b):
            return tuple(jnp.where(place >= 8 - by, 0.0, pltpu.roll(vk + apply(mk(), bk), 8 - by, axis=1))
                         for vk, mk, bk in zip(v, m, b))

        return lax.fori_loop(0, count, one, tuple(jnp.zeros((V, 8, 128), F32) for _ in v))

    def held(ref, *at_):
        return lambda: ref[at_].reshape(V, V, 8, 128)

    in_yi.wait()

    def turn_yi(j, _):
        yi_t[j] = turned(yi_v, j)
        return 0

    lax.fori_loop(0, CY, turn_yi, 0)

    received(xm_in, xm_rs, XO * XM, CHIPS)
    for e in range(3 * E):
        xmat[e // E, e % E] = xm_in[pl.ds(e, 8, stride=XM), :]
    received(xv_in, xv_rs, XO * XV, CHIPS)

    def rows_of(ref, first, stride):
        return jnp.stack([ref[pl.ds(first + c, 8, stride=stride), :] for c in range(V)])

    a, = chain([held(xmat, 0)], [rows_of(xv_in, 0, XV)], XO, CHIPS - 1)
    b, = chain_back([held(xmat, 2)], [rows_of(xv_in, V, XV) - apply(held(xmat, 1)(), a)], XO, CHIPS - 1)
    for c in range(V):
        xr_out[pl.ds(c, 8, stride=XV), :] = a[c]
        xr_out[pl.ds(V + c, 8, stride=XV), :] = b[c]
    own = CHIPS * core + chip
    pltpu.make_async_copy(at(xr_out, chip, XO * XV), at(xr_in, own, XO * XV), xr_rs.at[own]).start()
    for k in (4, 5, 2, 3, 6, 7, 1):
        x_back(k).start()
    pairs[1].wait()
    received(xr_in, xr_rs, XO * XV, NPX)

    before, after = [], []
    for h in range(2):
        a, b = rows_of(xr_in, 8 * h * XV, XV), rows_of(xr_in, 8 * h * XV + V, XV)

        def of(d, k, h=h):
            return pm[d, h, pl.ds(k * E, E)].reshape(V, V, 8, 128)

        a1 = part(0, h, 0) + apply(of(0, 0), a)
        b0 = part(1, h, 1) - apply(of(1, 1), a1) + apply(of(1, 2), b)
        before.append(jnp.where(core == 0, a, a1))
        after.append(jnp.where(core == 0, b0, b))

    def load_sx(i, h):
        return sx[:, x_rows(i, h), :]

    forward_cells(load_sx, x_block(xl_v), CX, tuple(before), save_fwx)
    backward_cells(load_fwx, x_block(xu_v), CX, tuple(after), save_fwx)

    def y_source(j, _):
        s = apply(yi_t[j], fwx[:, y_rows(j), :])
        sy[j] = s
        return s

    def save_fwy(j, _, f):
        fwy[j] = f

    def load_fwy(j, _):
        return fwy[j]

    end, = forward_cells(y_source, y_block(yl_t), CY, (None,), save_fwy)
    start, = backward_cells(load_fwy, y_block(yu_t), CY, (None,), None)
    for c in range(V):
        yv_out[pl.ds(c, 8, stride=YVP), :] = end[c]
        yv_out[pl.ds(V + c, 8, stride=YVP), :] = start[c]
    y_send(*yv)

    def y_back(d):
        return pltpu.make_async_remote_copy(
            at(yr_out, slot(d), YV, YVP), at(yr_in, z, YV, YVP), yr_ss.at[d], yr_rs.at[z], device_id=(px, d), device_id_type=MESH)

    @pl.when(is_owner)
    def _():
        received(ym_in, ym_rs, YM, NPY, YMP)
        for d in range(IN_Z):
            for e in range(3 * E):
                ymat[d, e // E, e % E] = ym_in[pl.ds(d * NPZ * YMP + e, 8, stride=YMP), :]
        mm, mz, mn = [[held(ymat, d, k) for d in range(IN_Z)] for k in range(3)]

        def keep(k, m):
            cmat[k] = m.reshape(E, 8, 128)

        phi = mm[0]()
        x = []
        for d in range(1, IN_Z):
            keep(3 + d, product(mz[d](), phi))
            phi = product(mm[d](), phi)
        keep(0, phi)
        x = held(cmat, 3 + IN_Z - 1)()
        for d in range(IN_Z - 2, 0, -1):
            x = held(cmat, 3 + d)() + product(mn[d](), x)
        keep(1, mz[0]() + product(mn[0](), x))
        n = mn[IN_Z - 1]()
        for d in range(IN_Z - 2, -1, -1):
            n = product(mn[d](), n)
        keep(2, n)

        received(yv_in, yv_rs, YV, NPY, YVP)
        v = [rows_of(yv_in, d * NPZ * YVP, YVP) for d in range(IN_Z)]
        w = [rows_of(yv_in, d * NPZ * YVP + V, YVP) for d in range(IN_Z)]
        e = v[0]
        ins = [None]
        for d in range(1, IN_Z):
            ins.append(e)
            e = v[d] + apply(mm[d](), e)
        g = w[IN_Z - 1] - apply(mz[IN_Z - 1](), ins[IN_Z - 1])
        for d in range(IN_Z - 2, -1, -1):
            g = w[d] + apply(mn[d](), g)
            if d:
                g = g - apply(mz[d](), ins[d])
        a, = chain([held(cmat, 0)], [e], 1, NPZ - 1)
        g = g - apply(held(cmat, 1)(), a)
        b, = chain_back([held(cmat, 2)], [g], 1, NPZ - 1)
        ins = [a]
        for d in range(IN_Z - 1):
            ins.append(v[d] + apply(mm[d](), ins[d]))
        ahead = [None] * IN_Z
        ahead[IN_Z - 1] = b
        for d in range(IN_Z - 1, 0, -1):
            ahead[d - 1] = w[d] - apply(mz[d](), ins[d]) + apply(mn[d](), ahead[d])
        for d in range(IN_Z):
            for c in range(V):
                yr_out[pl.ds(d * NPZ * YVP + c, 8, stride=YVP), :] = ins[d][c]
                yr_out[pl.ds(d * NPZ * YVP + V + c, 8, stride=YVP), :] = ahead[d][c]

        for dz in (4, 3, 5, 2, 6, 1, 7, 0):
            for dy in (2, 1, 3, 0):
                if dz or dy:
                    y_back(IN_Z * lax.rem(z + dz, NPZ) + lax.rem(py + dy, IN_Z)).start()
        pltpu.make_async_copy(at(yr_out, slot(py), YV, YVP), at(yr_in, z, YV, YVP), yr_rs.at[z]).start()

    received(yr_in, yr_rs, YV, NPZ, YVP)

    def load_sy(j, _):
        return sy[j]

    def save_res(j, _, u):
        out[:, y_rows(j), :] = u

    forward_cells(load_sy, y_block(yl_t), CY, (rows_of(yr_in, 0, YVP),), save_fwy)
    backward_cells(load_fwy, y_block(yu_t), CY, (rows_of(yr_in, V, YVP),), save_res)

    x_sent(*xm)
    x_sent(*xv)
    for k in range(1, NPX):
        x_back(k).wait_send()
    y_sent(*ym)
    y_sent(*yv)

    @pl.when(is_owner)
    def _():
        def one(k, _):
            y_back(lax.rem(py + k, NPY)).wait_send()
            return 0

        lax.fori_loop(1, NPY, one, 0)


def per_device(field, forcing, *blocks):
    shape = field.shape
    args = [v.reshape(V, ROWS, 128) for v in (field, forcing)] + [m.reshape(E, ROWS, 128) for m in blocks[:3]]
    args += [m.reshape(E, CX, CY, 128) for m in blocks[3:]]

    def vmem(*dims):
        return pltpu.VMEM(dims, F32)

    def dma(n):
        return pltpu.SemaphoreType.DMA((n,))

    scratch = [
        vmem(V, ROWS + 4 * CY, 128), vmem(V, ROWS, 128), *[vmem(E, ROWS, 128) for _ in range(3)],
        *[vmem(E, CX, YP, 128) for _ in range(3)], *[vmem(CY, V, V, 8, 128) for _ in range(3)],
        vmem(CY + 4, V, 8, 128), vmem(2, V, 2 * CY, 128), vmem(2, 2, V, 8, 128), vmem(V, ROWS, 128),
        vmem(CY, V, V, 8, 128), vmem(V, ROWS, 128), vmem(V, ROWS, 128), vmem(CY, V, 8, 128), vmem(CY, V, 8, 128),
        vmem(2, 2, 3 * E, 8, 128), vmem(2, 2, 2 * V, 8, 128), vmem(8 * XM, 128), vmem(8 * XM, 128),
        vmem(8 * XV, 128), vmem(8 * XV, 128), vmem(8 * XV, 128), vmem(CY * XV, 128),
        vmem(CX * YMP, 128), vmem(NPY * YMP, 128),
        vmem(CX * YVP, 128), vmem(NPY * YVP, 128), vmem(NPY * YVP, 128), vmem(CX * YVP, 128),
        vmem(3, E, 8, 128), vmem(IN_Z, 3, E, 8, 128), vmem(3 + IN_Z, E, 8, 128),
        dma(8), dma(4), dma(4), dma(3), dma(3), dma(CHIPS), dma(CHIPS), dma(CHIPS), dma(CHIPS), dma(NPX), dma(NPX),
        dma(NPZ), dma(NPY), dma(NPZ), dma(NPY), dma(NPY), dma(NPZ),
    ]
    result = pl.pallas_call(
        kernel,
        out_shape=jax.ShapeDtypeStruct((V, ROWS, 128), F32),
        in_specs=[pl.BlockSpec(memory_space=pltpu.HBM)] * 8,
        out_specs=pl.BlockSpec(memory_space=pltpu.VMEM),
        scratch_shapes=scratch,
        compiler_params=pltpu.CompilerParams(collective_id=0, has_side_effects=True, vmem_limit_bytes=56000000),
        name="adi",
    )(*args)
    return result.reshape(shape)


def solution(mesh):
    vector, matrix = P(None, "px", "py", None), P(None, None, "px", "py", None)
    return jax.shard_map(
        per_device, mesh=mesh, in_specs=(vector,) * 2 + (matrix,) * 6, out_specs=vector, check_vma=False
    )
```

```python
import jax
import jax.numpy as jnp
from jax import lax
from jax.experimental import pallas as pl
from jax.experimental.pallas import tpu as pltpu
from jax.sharding import PartitionSpec as P

DISSIPATION = 0.1
MESH = pl.DeviceIdType.MESH
F32 = jnp.float32

V = 5
E = V * V
NPX, NPY, NPZ = 8, 32, 8
IN_Z = NPY // NPZ
CX, CY = 8, 16
ROWS = CX * CY
XM, YM = 76, 75
XV, YV = 12, 10
YMP, YVP, YP = 88, 24, 24
CHIPS = NPX // 2
XO = CY // NPX


def block(ref, rows):
    return ref[:, rows, :].reshape(V, V, 8, 128)


def total(terms):
    while len(terms) > 1:
        terms = [terms[k] + terms[k + 1] if k + 1 < len(terms) else terms[k] for k in range(0, len(terms), 2)]
    return terms[0]


def apply(m, x):
    return total([m[:, c] * x[c][None] for c in range(V)])


def product(m, b):
    rows = [total([m[a, c][None] * b[c] for c in range(V)]) for a in range(V)]
    return jnp.stack(rows)


def device_products(lo, up, up_again, n, psi, emit, before_up=lambda: None):
    first = lo(0)
    psi[0] = first

    def forward(i, m):
        m = product(lo(i), m)
        psi[i] = m
        return m

    last = lax.fori_loop(1, n, forward, first)
    emit(0, last)
    before_up()

    def backward(t, z):
        i = n - 2 - t
        return psi[i] + product(up(i), z)

    emit(E, lax.fori_loop(0, n - 1, backward, last))

    def upward(t, m):
        return product(up_again(n - 2 - t), m)

    emit(2 * E, lax.fori_loop(0, n - 1, upward, up(n - 1)))


def forward_cells(source, lo, n, start, save):
    def step(i, carry):
        out = []
        for t, f in enumerate(carry):
            cur = source(i, t)
            if f is not None:
                cur = cur - apply(lo(i, t), f)
            save(i, t, cur)
            out.append(cur)
        return tuple(out)

    begin = 0
    if start[0] is None:
        start, begin = step(0, start), 1
    return lax.fori_loop(begin, n, step, start)


def backward_cells(source, up, n, start, save):
    def step(k, carry):
        i = n - 1 - k
        out = []
        for t, g in enumerate(carry):
            cur = source(i, t)
            if g is not None:
                cur = cur - apply(up(i, t), g)
            if save is not None:
                save(i, t, cur)
            out.append(cur)
        return tuple(out)

    begin = 0
    if start[0] is None:
        start, begin = step(0, start), 1
    return lax.fori_loop(begin, n, step, start)


def kernel(field, forcing, xi, xl, xu, yi, yl, yu, out,
           fx, fo, xi_v, xl_v, xu_v, yi_v, yl_v, yu_v, yi_t, yl_t, yu_t,
           fy, hx, hy, rhs, psi, sx, fwx, sy, fwy,
           pm, pv, xm_out, xm_in, xv_out, xv_in, xr_out, xr_in,
           ym_out, ym_in, yv_out, yv_in, yr_out, yr_in, xmat, ymat, cmat,
           load_s, halo_ss, halo_rs, pair_ss, pair_rs, xm_ss, xm_rs, xv_ss, xv_rs, xr_ss, xr_rs,
           ym_ss, ym_rs, yv_ss, yv_rs, yr_ss, yr_rs):
    px, py = lax.axis_index("px"), lax.axis_index("py")
    core, chip, z = lax.rem(px, 2), lax.div(px, 2), lax.div(py, IN_Z)
    partner = px + 1 - 2 * core

    def owner_of(r):
        return IN_Z * r + lax.rem(2 * core + r, IN_Z)

    is_owner = py == owner_of(z)

    mine = slice(2 * CY, 2 * CY + ROWS)

    def load(k, src, dst):
        return pltpu.make_async_copy(src, dst, load_s.at[k])

    padded = (slice(None), slice(None), slice(0, CY))
    in_xl, in_xu, in_field = load(0, xl, xl_v), load(1, xu, xu_v), load(2, field, fx.at[:, mine, :])
    in_yl, in_yu, in_yi = load(3, yl, yl_v.at[padded]), load(4, yu, yu_v.at[padded]), load(5, yi, yi_v.at[padded])
    in_fo, in_xi = load(6, forcing, fo), load(7, xi, xi_v)
    for c in (in_xl, in_xu, in_field):
        c.start()

    barrier = pltpu.get_barrier_semaphore()

    for dz in (4, 3, 5, 2, 6, 1, 7, 0):
        for dy in (2, 1, 3, 0):
            if dz or dy:
                other = IN_Z * lax.rem(z + dz, NPZ) + lax.rem(py + dy, IN_Z)
                pl.semaphore_signal(barrier, inc=1, device_id=(px, other), device_id_type=MESH)
    for k in (4, 5, 3, 2, 6, 1, 7):
        pl.semaphore_signal(barrier, inc=1, device_id=(lax.rem(px + k, NPX), py), device_id_type=MESH)

    def x_rows(i, h):
        return pl.ds(pl.multiple_of(CY * i + 8 * h, 8), 8)

    def y_rows(j):
        return pl.ds(j, 8, stride=CY)

    def turned(ref, j):
        return ref.reshape(E, CX * YP, 128)[:, pl.ds(j, 8, stride=YP), :].reshape(V, V, 8, 128)

    def x_block(ref):
        return lambda i, h: block(ref, x_rows(i, h))

    def y_block(ref):
        return lambda j, _=0: ref[j]

    def at(ref, k, size, pitch=None):
        return ref.at[pl.ds(pl.multiple_of(k * (pitch or size), 8), size), :]

    def x_copy(src, dst, ss, rs, size, c):
        return pltpu.make_async_remote_copy(
            at(src, c, size), at(dst, chip, size), ss.at[c], rs.at[chip],
            device_id=(2 * c + core, py), device_id_type=MESH)

    def other_chip(k):
        return lax.rem(chip + k, CHIPS)

    def x_send(src, dst, ss, rs, size):
        for k in (2, 1, 3):
            x_copy(src, dst, ss, rs, size, other_chip(k)).start()
        pltpu.make_async_copy(at(src, chip, size), at(dst, chip, size), rs.at[chip]).start()

    def x_sent(src, dst, ss, rs, size):
        for k in range(1, CHIPS):
            x_copy(src, dst, ss, rs, size, other_chip(k)).wait_send()

    def x_back(k):
        d = 2 * other_chip(k // 2) + lax.rem(core + k, 2)
        return pltpu.make_async_remote_copy(
            at(xr_out, lax.div(d, 2), XO * XV), at(xr_in, CHIPS * core + chip, XO * XV), xr_ss.at[d],
            xr_rs.at[CHIPS * core + chip], device_id=(d, py), device_id_type=MESH)

    def pair_copy(k, ref):
        return pltpu.make_async_remote_copy(
            ref, ref, pair_ss.at[k], pair_rs.at[k], device_id=(partner, py), device_id_type=MESH)

    pairs = [pair_copy(0, pm.at[core, 1 - core]), pair_copy(1, pm.at[core, core]), pair_copy(2, pv.at[core])]

    def received(dst, rs, size, count, pitch=None):
        def one(k, _):
            pltpu.make_async_copy(at(dst, k, size, pitch), at(dst, k, size, pitch), rs.at[k]).wait()
            return 0

        lax.fori_loop(0, count, one, 0)

    def slot(d):
        return NPZ * lax.rem(d, IN_Z) + lax.div(d, IN_Z)

    def y_copy(src, dst, ss, rs, size, pitch, r):
        return pltpu.make_async_remote_copy(
            at(src, r, size, pitch), at(dst, slot(py), size, pitch), ss.at[r], rs.at[slot(py)],
            device_id=(px, owner_of(r)), device_id_type=MESH)

    def y_send(src, dst, ss, rs, size, pitch):
        for k in (4, 3, 5, 2, 6, 1, 7):
            y_copy(src, dst, ss, rs, size, pitch, lax.rem(z + k, NPZ)).start()

        @pl.when(is_owner)
        def _():
            pltpu.make_async_copy(at(src, z, size, pitch), at(dst, slot(py), size, pitch), rs.at[slot(py)]).start()

        @pl.when(jnp.logical_not(is_owner))
        def _():
            y_copy(src, dst, ss, rs, size, pitch, z).start()

    def y_sent(src, dst, ss, rs, size, pitch):
        @pl.when(jnp.logical_not(is_owner))
        def _():
            y_copy(src, dst, ss, rs, size, pitch, z).wait_send()

        def one(k, _):
            y_copy(src, dst, ss, rs, size, pitch, lax.rem(z + k, NPZ)).wait_send()
            return 0

        lax.fori_loop(1, NPZ, one, 0)

    xm = (xm_out, xm_in, xm_ss, xm_rs, XO * XM)
    xv = (xv_out, xv_in, xv_ss, xv_rs, XO * XV)
    ym = (ym_out, ym_in, ym_ss, ym_rs, YM, YMP)
    yv = (yv_out, yv_in, yv_ss, yv_rs, YV, YVP)
    in_field.wait()

    def turn(j, _):
        fy[2 + j] = fx[:, pl.ds(2 * CY + j, 8, stride=CY), :]
        return 0

    lax.fori_loop(0, CY, turn, 0)

    right, left = lax.rem(px + 1, NPX), lax.rem(px + NPX - 1, NPX)
    north, south = lax.rem(py + 1, NPY), lax.rem(py + NPY - 1, NPY)
    halos = [
        pltpu.make_async_remote_copy(a, b, halo_ss.at[k], halo_rs.at[k], device_id=d, device_id_type=MESH)
        for k, (a, b, d) in enumerate([
            (fx.at[:, ROWS : ROWS + 2 * CY, :], hx.at[0], (right, py)),
            (fx.at[:, 2 * CY : 4 * CY, :], hx.at[1], (left, py)),
            (fy.at[CY : CY + 2], hy.at[0], (px, north)),
            (fy.at[2:4], hy.at[1], (px, south))])
    ]
    in_xl.wait()
    in_yl.start()
    in_yu.start()
    for first, h in ((True, 1 - core), (False, core)):
        def emit(base, m, h=h):
            pm[core, h, pl.ds(base, E)] = m.reshape(E, 8, 128)

        def before_up(first=first):
            if first:
                in_xu.wait()
                for c in (in_fo, in_xi, in_yi):
                    c.start()

        lo, up = [lambda i, ref=ref, h=h: block(ref, x_rows(i, h)) for ref in (xl_v, xu_v)]
        device_products(lo, up, up, CX, psi, emit, before_up)
        if first:
            pl.semaphore_wait(barrier, NPX + NPY - 2)
            pairs[0].start()
            for c in halos:
                c.start()
        else:
            pairs[1].start()

    in_yl.wait()

    def emit_y(base, m):
        for e in range(E):
            ym_out[pl.ds(base + e, 8, stride=YMP), :] = m[e // V, e % V]

    def lo_y(j):
        m = turned(yl_v, j)
        yl_t[j] = m
        return m

    def up_y(j):
        m = turned(yu_v, j)
        yu_t[j] = m
        return m

    device_products(lo_y, up_y, y_block(yu_t), CY, psi, emit_y, in_yu.wait)
    y_send(*ym)

    pairs[0].wait()

    def half(d, k):
        return pm[d, core, pl.ds(k * E, E)].reshape(V, V, 8, 128)

    def emit_x(base, m):
        for e in range(E):
            xm_out[pl.ds(base + e, 8, stride=XM), :] = m[e // V, e % V]

    m0, n0 = half(0, 0), half(0, 2)
    emit_x(0, product(half(1, 0), m0))
    emit_x(E, half(0, 1) + product(n0, product(half(1, 1), m0)))
    emit_x(2 * E, product(n0, half(1, 2)))
    x_send(*xm)

    in_fo.wait()
    for c in halos:
        c.wait()
    fx[:, 0 : 2 * CY, :] = jnp.where(px == 0, 0.0, hx[0])
    fx[:, 2 * CY + ROWS :, :] = jnp.where(px == NPX - 1, 0.0, hx[1])
    fy[0:2] = jnp.where(py == 0, 0.0, hy[0])
    fy[CY + 2 :] = jnp.where(py == NPY - 1, 0.0, hy[1])

    def difference(v):
        return v[0] - 4.0 * v[1] + 6.0 * v[2] - 4.0 * v[3] + v[4]

    def along_y(j, _):
        d = difference([fy[j + k] for k in range(5)])
        rhs[:, y_rows(j), :] = fo[:, y_rows(j), :] - DISSIPATION * d
        return 0

    lax.fori_loop(0, CY, along_y, 0)
    in_xi.wait()

    def x_source(i, h):
        d = difference([fx[:, x_rows(i + k, h), :] for k in range(5)])
        s = apply(block(xi_v, x_rows(i, h)), rhs[:, x_rows(i, h), :] - DISSIPATION * d)
        sx[:, x_rows(i, h), :] = s
        return s

    def save_fwx(i, h, f):
        fwx[:, x_rows(i, h), :] = f

    def load_fwx(i, h):
        return fwx[:, x_rows(i, h), :]

    ends = forward_cells(x_source, x_block(xl_v), CX, (None, None), save_fwx)
    starts = backward_cells(load_fwx, x_block(xu_v), CX, (None, None), None)
    for h in range(2):
        pv[core, h, pl.ds(0, V)] = ends[h]
        pv[core, h, pl.ds(V, V)] = starts[h]
    pairs[2].start()

    pairs[2].wait()

    def part(d, h, k):
        return pv[d, h, pl.ds(k * V, V)]

    v0 = part(0, core, 0)
    v = part(1, core, 0) + apply(half(1, 0), v0)
    w = part(0, core, 1) + apply(half(0, 2), part(1, core, 1) - apply(half(1, 1), v0))
    for c in range(V):
        xv_out[pl.ds(c, 8, stride=XV), :] = v[c]
        xv_out[pl.ds(V + c, 8, stride=XV), :] = w[c]
    x_send(*xv)

    place = lax.broadcasted_iota(jnp.int32, (V, 8, 128), 1)

    def chain(m, v, by, count):
        def one(_, a):
            return tuple(jnp.where(place < by, 0.0, pltpu.roll(vk + apply(mk(), ak), by, axis=1))
                         for vk, mk, ak in zip(v, m, a))

        return lax.fori_loop(0, count, one, tuple(jnp.zeros((V, 8, 128), F32) for _ in v))

    def chain_back(m, v, by, count):
        def one(_, b):
            return tuple(jnp.where(place >= 8 - by, 0.0, pltpu.roll(vk + apply(mk(), bk), 8 - by, axis=1))
                         for vk, mk, bk in zip(v, m, b))

        return lax.fori_loop(0, count, one, tuple(jnp.zeros((V, 8, 128), F32) for _ in v))

    def held(ref, *at_):
        return lambda: ref[at_].reshape(V, V, 8, 128)

    in_yi.wait()

    def turn_yi(j, _):
        yi_t[j] = turned(yi_v, j)
        return 0

    lax.fori_loop(0, CY, turn_yi, 0)

    received(xm_in, xm_rs, XO * XM, CHIPS)
    for e in range(3 * E):
        xmat[e // E, e % E] = xm_in[pl.ds(e, 8, stride=XM), :]
    received(xv_in, xv_rs, XO * XV, CHIPS)

    def rows_of(ref, first, stride):
        return jnp.stack([ref[pl.ds(first + c, 8, stride=stride), :] for c in range(V)])

    a, = chain([held(xmat, 0)], [rows_of(xv_in, 0, XV)], XO, CHIPS - 1)
    b, = chain_back([held(xmat, 2)], [rows_of(xv_in, V, XV) - apply(held(xmat, 1)(), a)], XO, CHIPS - 1)
    for c in range(V):
        xr_out[pl.ds(c, 8, stride=XV), :] = a[c]
        xr_out[pl.ds(V + c, 8, stride=XV), :] = b[c]
    own = CHIPS * core + chip
    pltpu.make_async_copy(at(xr_out, chip, XO * XV), at(xr_in, own, XO * XV), xr_rs.at[own]).start()
    for k in (4, 5, 2, 3, 6, 7, 1):
        x_back(k).start()
    pairs[1].wait()
    received(xr_in, xr_rs, XO * XV, NPX)

    before, after = [], []
    for h in range(2):
        a, b = rows_of(xr_in, 8 * h * XV, XV), rows_of(xr_in, 8 * h * XV + V, XV)

        def of(d, k, h=h):
            return pm[d, h, pl.ds(k * E, E)].reshape(V, V, 8, 128)

        a1 = part(0, h, 0) + apply(of(0, 0), a)
        b0 = part(1, h, 1) - apply(of(1, 1), a1) + apply(of(1, 2), b)
        before.append(jnp.where(core == 0, a, a1))
        after.append(jnp.where(core == 0, b0, b))

    def load_sx(i, h):
        return sx[:, x_rows(i, h), :]

    forward_cells(load_sx, x_block(xl_v), CX, tuple(before), save_fwx)
    backward_cells(load_fwx, x_block(xu_v), CX, tuple(after), save_fwx)

    def y_source(j, _):
        s = apply(yi_t[j], fwx[:, y_rows(j), :])
        sy[j] = s
        return s

    def save_fwy(j, _, f):
        fwy[j] = f

    def load_fwy(j, _):
        return fwy[j]

    end, = forward_cells(y_source, y_block(yl_t), CY, (None,), save_fwy)
    start, = backward_cells(load_fwy, y_block(yu_t), CY, (None,), None)
    for c in range(V):
        yv_out[pl.ds(c, 8, stride=YVP), :] = end[c]
        yv_out[pl.ds(V + c, 8, stride=YVP), :] = start[c]
    y_send(*yv)

    def y_back(d):
        return pltpu.make_async_remote_copy(
            at(yr_out, slot(d), YV, YVP), at(yr_in, z, YV, YVP), yr_ss.at[d], yr_rs.at[z], device_id=(px, d), device_id_type=MESH)

    @pl.when(is_owner)
    def _():
        received(ym_in, ym_rs, YM, NPY, YMP)
        for d in range(IN_Z):
            for e in range(3 * E):
                ymat[d, e // E, e % E] = ym_in[pl.ds(d * NPZ * YMP + e, 8, stride=YMP), :]
        mm, mz, mn = [[held(ymat, d, k) for d in range(IN_Z)] for k in range(3)]

        def keep(k, m):
            cmat[k] = m.reshape(E, 8, 128)

        phi = mm[0]()
        x = []
        for d in range(1, IN_Z):
            keep(3 + d, product(mz[d](), phi))
            phi = product(mm[d](), phi)
        keep(0, phi)
        x = held(cmat, 3 + IN_Z - 1)()
        for d in range(IN_Z - 2, 0, -1):
            x = held(cmat, 3 + d)() + product(mn[d](), x)
        keep(1, mz[0]() + product(mn[0](), x))
        n = mn[IN_Z - 1]()
        for d in range(IN_Z - 2, -1, -1):
            n = product(mn[d](), n)
        keep(2, n)

        received(yv_in, yv_rs, YV, NPY, YVP)
        v = [rows_of(yv_in, d * NPZ * YVP, YVP) for d in range(IN_Z)]
        w = [rows_of(yv_in, d * NPZ * YVP + V, YVP) for d in range(IN_Z)]
        e = v[0]
        ins = [None]
        for d in range(1, IN_Z):
            ins.append(e)
            e = v[d] + apply(mm[d](), e)
        g = w[IN_Z - 1] - apply(mz[IN_Z - 1](), ins[IN_Z - 1])
        for d in range(IN_Z - 2, -1, -1):
            g = w[d] + apply(mn[d](), g)
            if d:
                g = g - apply(mz[d](), ins[d])
        a, = chain([held(cmat, 0)], [e], 1, NPZ - 1)
        g = g - apply(held(cmat, 1)(), a)
        b, = chain_back([held(cmat, 2)], [g], 1, NPZ - 1)
        ins = [a]
        for d in range(IN_Z - 1):
            ins.append(v[d] + apply(mm[d](), ins[d]))
        ahead = [None] * IN_Z
        ahead[IN_Z - 1] = b
        for d in range(IN_Z - 1, 0, -1):
            ahead[d - 1] = w[d] - apply(mz[d](), ins[d]) + apply(mn[d](), ahead[d])
        for d in range(IN_Z):
            for c in range(V):
                yr_out[pl.ds(d * NPZ * YVP + c, 8, stride=YVP), :] = ins[d][c]
                yr_out[pl.ds(d * NPZ * YVP + V + c, 8, stride=YVP), :] = ahead[d][c]

        for dz in (4, 3, 5, 2, 6, 1, 7, 0):
            for dy in (2, 1, 3, 0):
                if dz or dy:
                    y_back(IN_Z * lax.rem(z + dz, NPZ) + lax.rem(py + dy, IN_Z)).start()
        pltpu.make_async_copy(at(yr_out, slot(py), YV, YVP), at(yr_in, z, YV, YVP), yr_rs.at[z]).start()

    x_sent(*xm)
    x_sent(*xv)
    for k in range(1, NPX):
        x_back(k).wait_send()
    y_sent(*ym)
    y_sent(*yv)

    @pl.when(is_owner)
    def _():
        def one(k, _):
            y_back(lax.rem(py + k, NPY)).wait_send()
            return 0

        lax.fori_loop(1, NPY, one, 0)

    received(yr_in, yr_rs, YV, NPZ, YVP)

    def load_sy(j, _):
        return sy[j]

    def save_res(j, _, u):
        out[:, y_rows(j), :] = u

    forward_cells(load_sy, y_block(yl_t), CY, (rows_of(yr_in, 0, YVP),), save_fwy)
    backward_cells(load_fwy, y_block(yu_t), CY, (rows_of(yr_in, V, YVP),), save_res)


def per_device(field, forcing, *blocks):
    shape = field.shape
    args = [v.reshape(V, ROWS, 128) for v in (field, forcing)] + [m.reshape(E, ROWS, 128) for m in blocks[:3]]
    args += [m.reshape(E, CX, CY, 128) for m in blocks[3:]]

    def vmem(*dims):
        return pltpu.VMEM(dims, F32)

    def dma(n):
        return pltpu.SemaphoreType.DMA((n,))

    scratch = [
        vmem(V, ROWS + 4 * CY, 128), vmem(V, ROWS, 128), *[vmem(E, ROWS, 128) for _ in range(3)],
        *[vmem(E, CX, YP, 128) for _ in range(3)], *[vmem(CY, V, V, 8, 128) for _ in range(3)],
        vmem(CY + 4, V, 8, 128), vmem(2, V, 2 * CY, 128), vmem(2, 2, V, 8, 128), vmem(V, ROWS, 128),
        vmem(CY, V, V, 8, 128), vmem(V, ROWS, 128), vmem(V, ROWS, 128), vmem(CY, V, 8, 128), vmem(CY, V, 8, 128),
        vmem(2, 2, 3 * E, 8, 128), vmem(2, 2, 2 * V, 8, 128), vmem(8 * XM, 128), vmem(8 * XM, 128),
        vmem(8 * XV, 128), vmem(8 * XV, 128), vmem(8 * XV, 128), vmem(CY * XV, 128),
        vmem(CX * YMP, 128), vmem(NPY * YMP, 128),
        vmem(CX * YVP, 128), vmem(NPY * YVP, 128), vmem(NPY * YVP, 128), vmem(CX * YVP, 128),
        vmem(3, E, 8, 128), vmem(IN_Z, 3, E, 8, 128), vmem(3 + IN_Z, E, 8, 128),
        dma(8), dma(4), dma(4), dma(3), dma(3), dma(CHIPS), dma(CHIPS), dma(CHIPS), dma(CHIPS), dma(NPX), dma(NPX),
        dma(NPZ), dma(NPY), dma(NPZ), dma(NPY), dma(NPY), dma(NPZ),
    ]
    result = pl.pallas_call(
        kernel,
        out_shape=jax.ShapeDtypeStruct((V, ROWS, 128), F32),
        in_specs=[pl.BlockSpec(memory_space=pltpu.HBM)] * 8,
        out_specs=pl.BlockSpec(memory_space=pltpu.VMEM),
        scratch_shapes=scratch,
        compiler_params=pltpu.CompilerParams(collective_id=0, has_side_effects=True, vmem_limit_bytes=56000000),
        name="adi",
    )(*args)
    return result.reshape(shape)


def solution(mesh):
    vector, matrix = P(None, "px", "py", None), P(None, None, "px", "py", None)
    return jax.shard_map(
        per_device, mesh=mesh, in_specs=(vector,) * 2 + (matrix,) * 6, out_specs=vector, check_vma=False
    )
```

```python
import jax
import jax.numpy as jnp
from jax import lax
from jax.experimental import pallas as pl
from jax.experimental.pallas import tpu as pltpu
from jax.sharding import PartitionSpec as P

DISSIPATION = 0.1
MESH = pl.DeviceIdType.MESH
F32 = jnp.float32

V = 5
UNROLL = 4
E = V * V
NPX, NPY, NPZ = 8, 32, 8
IN_Z = NPY // NPZ
CX, CY = 8, 16
ROWS = CX * CY
XM, YM = 76, 75
XV, YV = 12, 10
YMP, YVP, YP = 88, 24, 24
CHIPS = NPX // 2
XO = CY // NPX


def block(ref, rows):
    return ref[:, rows, :].reshape(V, V, 8, 128)


def total(terms):
    while len(terms) > 1:
        terms = [terms[k] + terms[k + 1] if k + 1 < len(terms) else terms[k] for k in range(0, len(terms), 2)]
    return terms[0]


def apply(m, x):
    return total([m[:, c] * x[c][None] for c in range(V)])


def product(m, b):
    rows = [total([m[a, c][None] * b[c] for c in range(V)]) for a in range(V)]
    return jnp.stack(rows)


def device_products(lo, up, up_again, n, psi, emit, before_up=lambda: None):
    first = lo(0)
    psi[0] = first

    def forward(i, m):
        m = product(lo(i), m)
        psi[i] = m
        return m

    last = lax.fori_loop(1, n, forward, first)
    emit(0, last)
    before_up()

    def backward(t, z):
        i = n - 2 - t
        return psi[i] + product(up(i), z)

    emit(E, lax.fori_loop(0, n - 1, backward, last))

    def upward(t, m):
        return product(up_again(n - 2 - t), m)

    emit(2 * E, lax.fori_loop(0, n - 1, upward, up(n - 1)))


def forward_cells(source, lo, n, start, save):
    def step(i, carry):
        out = []
        for t, f in enumerate(carry):
            cur = source(i, t)
            if f is not None:
                cur = cur - apply(lo(i, t), f)
            save(i, t, cur)
            out.append(cur)
        return tuple(out)

    begin = 0
    if start[0] is None:
        start, begin = step(0, start), 1
    return lax.fori_loop(begin, n, step, start, unroll=UNROLL)


def backward_cells(source, up, n, start, save):
    def step(k, carry):
        i = n - 1 - k
        out = []
        for t, g in enumerate(carry):
            cur = source(i, t)
            if g is not None:
                cur = cur - apply(up(i, t), g)
            if save is not None:
                save(i, t, cur)
            out.append(cur)
        return tuple(out)

    begin = 0
    if start[0] is None:
        start, begin = step(0, start), 1
    return lax.fori_loop(begin, n, step, start, unroll=UNROLL)


def kernel(field, forcing, xi, xl, xu, yi, yl, yu, out,
           fx, fo, xi_v, xl_v, xu_v, yi_v, yl_v, yu_v, yi_t, yl_t, yu_t,
           fy, hx, hy, rhs, psi, sx, fwx, sy, fwy,
           pm, pv, xm_out, xm_in, xv_out, xv_in, xr_out, xr_in,
           ym_out, ym_in, yv_out, yv_in, yr_out, yr_in, xmat, ymat, cmat,
           load_s, halo_ss, halo_rs, pair_ss, pair_rs, xm_ss, xm_rs, xv_ss, xv_rs, xr_ss, xr_rs,
           ym_ss, ym_rs, yv_ss, yv_rs, yr_ss, yr_rs):
    px, py = lax.axis_index("px"), lax.axis_index("py")
    core, chip, z = lax.rem(px, 2), lax.div(px, 2), lax.div(py, IN_Z)
    partner = px + 1 - 2 * core

    def owner_of(r):
        return IN_Z * r + lax.rem(2 * core + r, IN_Z)

    is_owner = py == owner_of(z)

    mine = slice(2 * CY, 2 * CY + ROWS)

    def load(k, src, dst):
        return pltpu.make_async_copy(src, dst, load_s.at[k])

    padded = (slice(None), slice(None), slice(0, CY))
    in_xl, in_xu, in_field = load(0, xl, xl_v), load(1, xu, xu_v), load(2, field, fx.at[:, mine, :])
    in_yl, in_yu, in_yi = load(3, yl, yl_v.at[padded]), load(4, yu, yu_v.at[padded]), load(5, yi, yi_v.at[padded])
    in_fo, in_xi = load(6, forcing, fo), load(7, xi, xi_v)
    for c in (in_xl, in_xu, in_field):
        c.start()

    barrier = pltpu.get_barrier_semaphore()

    for dz in (4, 3, 5, 2, 6, 1, 7, 0):
        for dy in (2, 1, 3, 0):
            if dz or dy:
                other = IN_Z * lax.rem(z + dz, NPZ) + lax.rem(py + dy, IN_Z)
                pl.semaphore_signal(barrier, inc=1, device_id=(px, other), device_id_type=MESH)
    for k in (4, 5, 3, 2, 6, 1, 7):
        pl.semaphore_signal(barrier, inc=1, device_id=(lax.rem(px + k, NPX), py), device_id_type=MESH)

    def x_rows(i, h):
        return pl.ds(pl.multiple_of(CY * i + 8 * h, 8), 8)

    def y_rows(j):
        return pl.ds(j, 8, stride=CY)

    def turned(ref, j):
        return ref.reshape(E, CX * YP, 128)[:, pl.ds(j, 8, stride=YP), :].reshape(V, V, 8, 128)

    def x_block(ref):
        return lambda i, h: block(ref, x_rows(i, h))

    def y_block(ref):
        return lambda j, _=0: ref[j]

    def at(ref, k, size, pitch=None):
        return ref.at[pl.ds(pl.multiple_of(k * (pitch or size), 8), size), :]

    def x_copy(src, dst, ss, rs, size, c):
        return pltpu.make_async_remote_copy(
            at(src, c, size), at(dst, chip, size), ss.at[c], rs.at[chip],
            device_id=(2 * c + core, py), device_id_type=MESH)

    def other_chip(k):
        return lax.rem(chip + k, CHIPS)

    def x_send(src, dst, ss, rs, size):
        for k in (2, 1, 3):
            x_copy(src, dst, ss, rs, size, other_chip(k)).start()
        pltpu.make_async_copy(at(src, chip, size), at(dst, chip, size), rs.at[chip]).start()

    def x_sent(src, dst, ss, rs, size):
        for k in range(1, CHIPS):
            x_copy(src, dst, ss, rs, size, other_chip(k)).wait_send()

    def x_back(k):
        d = 2 * other_chip(k // 2) + lax.rem(core + k, 2)
        return pltpu.make_async_remote_copy(
            at(xr_out, lax.div(d, 2), XO * XV), at(xr_in, CHIPS * core + chip, XO * XV), xr_ss.at[d],
            xr_rs.at[CHIPS * core + chip], device_id=(d, py), device_id_type=MESH)

    def pair_copy(k, ref):
        return pltpu.make_async_remote_copy(
            ref, ref, pair_ss.at[k], pair_rs.at[k], device_id=(partner, py), device_id_type=MESH)

    pairs = [pair_copy(0, pm.at[core, 1 - core]), pair_copy(1, pm.at[core, core]), pair_copy(2, pv.at[core])]

    def received(dst, rs, size, count, pitch=None):
        def one(k, _):
            pltpu.make_async_copy(at(dst, k, size, pitch), at(dst, k, size, pitch), rs.at[k]).wait()
            return 0

        lax.fori_loop(0, count, one, 0)

    def slot(d):
        return NPZ * lax.rem(d, IN_Z) + lax.div(d, IN_Z)

    def y_copy(src, dst, ss, rs, size, pitch, r):
        return pltpu.make_async_remote_copy(
            at(src, r, size, pitch), at(dst, slot(py), size, pitch), ss.at[r], rs.at[slot(py)],
            device_id=(px, owner_of(r)), device_id_type=MESH)

    def y_send(src, dst, ss, rs, size, pitch):
        for k in (4, 3, 5, 2, 6, 1, 7):
            y_copy(src, dst, ss, rs, size, pitch, lax.rem(z + k, NPZ)).start()

        @pl.when(is_owner)
        def _():
            pltpu.make_async_copy(at(src, z, size, pitch), at(dst, slot(py), size, pitch), rs.at[slot(py)]).start()

        @pl.when(jnp.logical_not(is_owner))
        def _():
            y_copy(src, dst, ss, rs, size, pitch, z).start()

    def y_sent(src, dst, ss, rs, size, pitch):
        @pl.when(jnp.logical_not(is_owner))
        def _():
            y_copy(src, dst, ss, rs, size, pitch, z).wait_send()

        def one(k, _):
            y_copy(src, dst, ss, rs, size, pitch, lax.rem(z + k, NPZ)).wait_send()
            return 0

        lax.fori_loop(1, NPZ, one, 0)

    xm = (xm_out, xm_in, xm_ss, xm_rs, XO * XM)
    xv = (xv_out, xv_in, xv_ss, xv_rs, XO * XV)
    ym = (ym_out, ym_in, ym_ss, ym_rs, YM, YMP)
    yv = (yv_out, yv_in, yv_ss, yv_rs, YV, YVP)
    in_field.wait()

    def turn(j, _):
        fy[2 + j] = fx[:, pl.ds(2 * CY + j, 8, stride=CY), :]
        return 0

    lax.fori_loop(0, CY, turn, 0)

    right, left = lax.rem(px + 1, NPX), lax.rem(px + NPX - 1, NPX)
    north, south = lax.rem(py + 1, NPY), lax.rem(py + NPY - 1, NPY)
    halos = [
        pltpu.make_async_remote_copy(a, b, halo_ss.at[k], halo_rs.at[k], device_id=d, device_id_type=MESH)
        for k, (a, b, d) in enumerate([
            (fx.at[:, ROWS : ROWS + 2 * CY, :], hx.at[0], (right, py)),
            (fx.at[:, 2 * CY : 4 * CY, :], hx.at[1], (left, py)),
            (fy.at[CY : CY + 2], hy.at[0], (px, north)),
            (fy.at[2:4], hy.at[1], (px, south))])
    ]
    in_xl.wait()
    in_yl.start()
    in_yu.start()
    for first, h in ((True, 1 - core), (False, core)):
        def emit(base, m, h=h):
            pm[core, h, pl.ds(base, E)] = m.reshape(E, 8, 128)

        def before_up(first=first):
            if first:
                in_xu.wait()
                for c in (in_fo, in_xi, in_yi):
                    c.start()

        lo, up = [lambda i, ref=ref, h=h: block(ref, x_rows(i, h)) for ref in (xl_v, xu_v)]
        device_products(lo, up, up, CX, psi, emit, before_up)
        if first:
            pl.semaphore_wait(barrier, NPX + NPY - 2)
            pairs[0].start()
            for c in halos:
                c.start()
        else:
            pairs[1].start()

    in_yl.wait()

    def emit_y(base, m):
        for e in range(E):
            ym_out[pl.ds(base + e, 8, stride=YMP), :] = m[e // V, e % V]

    def lo_y(j):
        m = turned(yl_v, j)
        yl_t[j] = m
        return m

    def up_y(j):
        m = turned(yu_v, j)
        yu_t[j] = m
        return m

    device_products(lo_y, up_y, y_block(yu_t), CY, psi, emit_y, in_yu.wait)
    y_send(*ym)

    pairs[0].wait()

    def half(d, k):
        return pm[d, core, pl.ds(k * E, E)].reshape(V, V, 8, 128)

    def emit_x(base, m):
        for e in range(E):
            xm_out[pl.ds(base + e, 8, stride=XM), :] = m[e // V, e % V]

    m0, n0 = half(0, 0), half(0, 2)
    emit_x(0, product(half(1, 0), m0))
    emit_x(E, half(0, 1) + product(n0, product(half(1, 1), m0)))
    emit_x(2 * E, product(n0, half(1, 2)))
    x_send(*xm)

    in_fo.wait()
    for c in halos:
        c.wait()
    fx[:, 0 : 2 * CY, :] = jnp.where(px == 0, 0.0, hx[0])
    fx[:, 2 * CY + ROWS :, :] = jnp.where(px == NPX - 1, 0.0, hx[1])
    fy[0:2] = jnp.where(py == 0, 0.0, hy[0])
    fy[CY + 2 :] = jnp.where(py == NPY - 1, 0.0, hy[1])

    def difference(v):
        return v[0] - 4.0 * v[1] + 6.0 * v[2] - 4.0 * v[3] + v[4]

    def along_y(j, _):
        d = difference([fy[j + k] for k in range(5)])
        rhs[:, y_rows(j), :] = fo[:, y_rows(j), :] - DISSIPATION * d
        return 0

    lax.fori_loop(0, CY, along_y, 0)
    in_xi.wait()

    def x_source(i, h):
        d = difference([fx[:, x_rows(i + k, h), :] for k in range(5)])
        s = apply(block(xi_v, x_rows(i, h)), rhs[:, x_rows(i, h), :] - DISSIPATION * d)
        sx[:, x_rows(i, h), :] = s
        return s

    def save_fwx(i, h, f):
        fwx[:, x_rows(i, h), :] = f

    def load_fwx(i, h):
        return fwx[:, x_rows(i, h), :]

    ends = forward_cells(x_source, x_block(xl_v), CX, (None, None), save_fwx)
    starts = backward_cells(load_fwx, x_block(xu_v), CX, (None, None), None)
    for h in range(2):
        pv[core, h, pl.ds(0, V)] = ends[h]
        pv[core, h, pl.ds(V, V)] = starts[h]
    pairs[2].start()

    pairs[2].wait()

    def part(d, h, k):
        return pv[d, h, pl.ds(k * V, V)]

    v0 = part(0, core, 0)
    v = part(1, core, 0) + apply(half(1, 0), v0)
    w = part(0, core, 1) + apply(half(0, 2), part(1, core, 1) - apply(half(1, 1), v0))
    for c in range(V):
        xv_out[pl.ds(c, 8, stride=XV), :] = v[c]
        xv_out[pl.ds(V + c, 8, stride=XV), :] = w[c]
    x_send(*xv)

    place = lax.broadcasted_iota(jnp.int32, (V, 8, 128), 1)

    def chain(m, v, by, count):
        def one(_, a):
            return tuple(jnp.where(place < by, 0.0, pltpu.roll(vk + apply(mk(), ak), by, axis=1))
                         for vk, mk, ak in zip(v, m, a))

        return lax.fori_loop(0, count, one, tuple(jnp.zeros((V, 8, 128), F32) for _ in v))

    def chain_back(m, v, by, count):
        def one(_, b):
            return tuple(jnp.where(place >= 8 - by, 0.0, pltpu.roll(vk + apply(mk(), bk), 8 - by, axis=1))
                         for vk, mk, bk in zip(v, m, b))

        return lax.fori_loop(0, count, one, tuple(jnp.zeros((V, 8, 128), F32) for _ in v))

    def held(ref, *at_):
        return lambda: ref[at_].reshape(V, V, 8, 128)

    in_yi.wait()

    def turn_yi(j, _):
        yi_t[j] = turned(yi_v, j)
        return 0

    lax.fori_loop(0, CY, turn_yi, 0)

    received(xm_in, xm_rs, XO * XM, CHIPS)
    for e in range(3 * E):
        xmat[e // E, e % E] = xm_in[pl.ds(e, 8, stride=XM), :]
    received(xv_in, xv_rs, XO * XV, CHIPS)

    def rows_of(ref, first, stride):
        return jnp.stack([ref[pl.ds(first + c, 8, stride=stride), :] for c in range(V)])

    a, = chain([held(xmat, 0)], [rows_of(xv_in, 0, XV)], XO, CHIPS - 1)
    b, = chain_back([held(xmat, 2)], [rows_of(xv_in, V, XV) - apply(held(xmat, 1)(), a)], XO, CHIPS - 1)
    for c in range(V):
        xr_out[pl.ds(c, 8, stride=XV), :] = a[c]
        xr_out[pl.ds(V + c, 8, stride=XV), :] = b[c]
    own = CHIPS * core + chip
    pltpu.make_async_copy(at(xr_out, chip, XO * XV), at(xr_in, own, XO * XV), xr_rs.at[own]).start()
    for k in (4, 5, 2, 3, 6, 7, 1):
        x_back(k).start()
    pairs[1].wait()
    received(xr_in, xr_rs, XO * XV, NPX)

    before, after = [], []
    for h in range(2):
        a, b = rows_of(xr_in, 8 * h * XV, XV), rows_of(xr_in, 8 * h * XV + V, XV)

        def of(d, k, h=h):
            return pm[d, h, pl.ds(k * E, E)].reshape(V, V, 8, 128)

        a1 = part(0, h, 0) + apply(of(0, 0), a)
        b0 = part(1, h, 1) - apply(of(1, 1), a1) + apply(of(1, 2), b)
        before.append(jnp.where(core == 0, a, a1))
        after.append(jnp.where(core == 0, b0, b))

    def load_sx(i, h):
        return sx[:, x_rows(i, h), :]

    forward_cells(load_sx, x_block(xl_v), CX, tuple(before), save_fwx)
    backward_cells(load_fwx, x_block(xu_v), CX, tuple(after), save_fwx)

    def y_source(j, _):
        s = apply(yi_t[j], fwx[:, y_rows(j), :])
        sy[j] = s
        return s

    def save_fwy(j, _, f):
        fwy[j] = f

    def load_fwy(j, _):
        return fwy[j]

    end, = forward_cells(y_source, y_block(yl_t), CY, (None,), save_fwy)
    start, = backward_cells(load_fwy, y_block(yu_t), CY, (None,), None)
    for c in range(V):
        yv_out[pl.ds(c, 8, stride=YVP), :] = end[c]
        yv_out[pl.ds(V + c, 8, stride=YVP), :] = start[c]
    y_send(*yv)

    def y_back(d):
        return pltpu.make_async_remote_copy(
            at(yr_out, slot(d), YV, YVP), at(yr_in, z, YV, YVP), yr_ss.at[d], yr_rs.at[z], device_id=(px, d), device_id_type=MESH)

    @pl.when(is_owner)
    def _():
        received(ym_in, ym_rs, YM, NPY, YMP)
        for d in range(IN_Z):
            for e in range(3 * E):
                ymat[d, e // E, e % E] = ym_in[pl.ds(d * NPZ * YMP + e, 8, stride=YMP), :]
        mm, mz, mn = [[held(ymat, d, k) for d in range(IN_Z)] for k in range(3)]

        def keep(k, m):
            cmat[k] = m.reshape(E, 8, 128)

        phi = mm[0]()
        x = []
        for d in range(1, IN_Z):
            keep(3 + d, product(mz[d](), phi))
            phi = product(mm[d](), phi)
        keep(0, phi)
        x = held(cmat, 3 + IN_Z - 1)()
        for d in range(IN_Z - 2, 0, -1):
            x = held(cmat, 3 + d)() + product(mn[d](), x)
        keep(1, mz[0]() + product(mn[0](), x))
        n = mn[IN_Z - 1]()
        for d in range(IN_Z - 2, -1, -1):
            n = product(mn[d](), n)
        keep(2, n)

        received(yv_in, yv_rs, YV, NPY, YVP)
        v = [rows_of(yv_in, d * NPZ * YVP, YVP) for d in range(IN_Z)]
        w = [rows_of(yv_in, d * NPZ * YVP + V, YVP) for d in range(IN_Z)]
        e = v[0]
        ins = [None]
        for d in range(1, IN_Z):
            ins.append(e)
            e = v[d] + apply(mm[d](), e)
        g = w[IN_Z - 1] - apply(mz[IN_Z - 1](), ins[IN_Z - 1])
        for d in range(IN_Z - 2, -1, -1):
            g = w[d] + apply(mn[d](), g)
            if d:
                g = g - apply(mz[d](), ins[d])
        a, = chain([held(cmat, 0)], [e], 1, NPZ - 1)
        g = g - apply(held(cmat, 1)(), a)
        b, = chain_back([held(cmat, 2)], [g], 1, NPZ - 1)
        ins = [a]
        for d in range(IN_Z - 1):
            ins.append(v[d] + apply(mm[d](), ins[d]))
        ahead = [None] * IN_Z
        ahead[IN_Z - 1] = b
        for d in range(IN_Z - 1, 0, -1):
            ahead[d - 1] = w[d] - apply(mz[d](), ins[d]) + apply(mn[d](), ahead[d])
        for d in range(IN_Z):
            for c in range(V):
                yr_out[pl.ds(d * NPZ * YVP + c, 8, stride=YVP), :] = ins[d][c]
                yr_out[pl.ds(d * NPZ * YVP + V + c, 8, stride=YVP), :] = ahead[d][c]

        for dz in (4, 3, 5, 2, 6, 1, 7, 0):
            for dy in (2, 1, 3, 0):
                if dz or dy:
                    y_back(IN_Z * lax.rem(z + dz, NPZ) + lax.rem(py + dy, IN_Z)).start()
        pltpu.make_async_copy(at(yr_out, slot(py), YV, YVP), at(yr_in, z, YV, YVP), yr_rs.at[z]).start()

    x_sent(*xm)
    x_sent(*xv)
    for k in range(1, NPX):
        x_back(k).wait_send()
    y_sent(*ym)
    y_sent(*yv)

    @pl.when(is_owner)
    def _():
        def one(k, _):
            y_back(lax.rem(py + k, NPY)).wait_send()
            return 0

        lax.fori_loop(1, NPY, one, 0)

    received(yr_in, yr_rs, YV, NPZ, YVP)

    def load_sy(j, _):
        return sy[j]

    def save_res(j, _, u):
        out[:, y_rows(j), :] = u

    forward_cells(load_sy, y_block(yl_t), CY, (rows_of(yr_in, 0, YVP),), save_fwy)
    backward_cells(load_fwy, y_block(yu_t), CY, (rows_of(yr_in, V, YVP),), save_res)


def per_device(field, forcing, *blocks):
    shape = field.shape
    args = [v.reshape(V, ROWS, 128) for v in (field, forcing)] + [m.reshape(E, ROWS, 128) for m in blocks[:3]]
    args += [m.reshape(E, CX, CY, 128) for m in blocks[3:]]

    def vmem(*dims):
        return pltpu.VMEM(dims, F32)

    def dma(n):
        return pltpu.SemaphoreType.DMA((n,))

    scratch = [
        vmem(V, ROWS + 4 * CY, 128), vmem(V, ROWS, 128), *[vmem(E, ROWS, 128) for _ in range(3)],
        *[vmem(E, CX, YP, 128) for _ in range(3)], *[vmem(CY, V, V, 8, 128) for _ in range(3)],
        vmem(CY + 4, V, 8, 128), vmem(2, V, 2 * CY, 128), vmem(2, 2, V, 8, 128), vmem(V, ROWS, 128),
        vmem(CY, V, V, 8, 128), vmem(V, ROWS, 128), vmem(V, ROWS, 128), vmem(CY, V, 8, 128), vmem(CY, V, 8, 128),
        vmem(2, 2, 3 * E, 8, 128), vmem(2, 2, 2 * V, 8, 128), vmem(8 * XM, 128), vmem(8 * XM, 128),
        vmem(8 * XV, 128), vmem(8 * XV, 128), vmem(8 * XV, 128), vmem(CY * XV, 128),
        vmem(CX * YMP, 128), vmem(NPY * YMP, 128),
        vmem(CX * YVP, 128), vmem(NPY * YVP, 128), vmem(NPY * YVP, 128), vmem(CX * YVP, 128),
        vmem(3, E, 8, 128), vmem(IN_Z, 3, E, 8, 128), vmem(3 + IN_Z, E, 8, 128),
        dma(8), dma(4), dma(4), dma(3), dma(3), dma(CHIPS), dma(CHIPS), dma(CHIPS), dma(CHIPS), dma(NPX), dma(NPX),
        dma(NPZ), dma(NPY), dma(NPZ), dma(NPY), dma(NPY), dma(NPZ),
    ]
    result = pl.pallas_call(
        kernel,
        out_shape=jax.ShapeDtypeStruct((V, ROWS, 128), F32),
        in_specs=[pl.BlockSpec(memory_space=pltpu.HBM)] * 8,
        out_specs=pl.BlockSpec(memory_space=pltpu.VMEM),
        scratch_shapes=scratch,
        compiler_params=pltpu.CompilerParams(collective_id=0, has_side_effects=True, vmem_limit_bytes=56000000),
        name="adi",
    )(*args)
    return result.reshape(shape)


def solution(mesh):
    vector, matrix = P(None, "px", "py", None), P(None, None, "px", "py", None)
    return jax.shard_map(
        per_device, mesh=mesh, in_specs=(vector,) * 2 + (matrix,) * 6, out_specs=vector, check_vma=False
    )
```

```python
import jax
import jax.numpy as jnp
from jax import lax
from jax.experimental import pallas as pl
from jax.experimental.pallas import tpu as pltpu
from jax.sharding import PartitionSpec as P

DISSIPATION = 0.1
MESH = pl.DeviceIdType.MESH
F32 = jnp.float32

V = 5
UNROLL = 4
E = V * V
NPX, NPY, NPZ = 8, 32, 8
IN_Z = NPY // NPZ
CX, CY = 8, 16
ROWS = CX * CY
XM, YM = 76, 75
XV, YV = 12, 10
YMP, YVP, YP = 88, 24, 24
CHIPS = NPX // 2
XO = CY // NPX


def block(ref, rows):
    return ref[:, rows, :].reshape(V, V, 8, 128)


def total(terms):
    while len(terms) > 1:
        terms = [terms[k] + terms[k + 1] if k + 1 < len(terms) else terms[k] for k in range(0, len(terms), 2)]
    return terms[0]


def apply(m, x):
    return total([m[:, c] * x[c][None] for c in range(V)])


def product(m, b):
    rows = [total([m[a, c][None] * b[c] for c in range(V)]) for a in range(V)]
    return jnp.stack(rows)


def device_products(lo, up, up_again, n, psi, emit, before_up=lambda: None):
    first = lo(0)
    psi[0] = first

    def forward(i, m):
        m = product(lo(i), m)
        psi[i] = m
        return m

    last = lax.fori_loop(1, n, forward, first)
    emit(0, last)
    before_up()

    def backward(t, z):
        i = n - 2 - t
        return psi[i] + product(up(i), z)

    emit(E, lax.fori_loop(0, n - 1, backward, last))

    def upward(t, m):
        return product(up_again(n - 2 - t), m)

    emit(2 * E, lax.fori_loop(0, n - 1, upward, up(n - 1)))


def forward_cells(source, lo, n, start, save):
    def step(i, carry):
        out = []
        for t, f in enumerate(carry):
            cur = source(i, t)
            if f is not None:
                cur = cur - apply(lo(i, t), f)
            save(i, t, cur)
            out.append(cur)
        return tuple(out)

    begin = 0
    if start[0] is None:
        start, begin = step(0, start), 1
    return lax.fori_loop(begin, n, step, start, unroll=UNROLL)


def backward_cells(source, up, n, start, save):
    def step(k, carry):
        i = n - 1 - k
        out = []
        for t, g in enumerate(carry):
            cur = source(i, t)
            if g is not None:
                cur = cur - apply(up(i, t), g)
            if save is not None:
                save(i, t, cur)
            out.append(cur)
        return tuple(out)

    begin = 0
    if start[0] is None:
        start, begin = step(0, start), 1
    return lax.fori_loop(begin, n, step, start, unroll=UNROLL)


def kernel(field, forcing, xi, xl, xu, yi, yl, yu, out,
           fx, fo, xi_v, xl_v, xu_v, yi_v, yl_v, yu_v, yi_t, yl_t, yu_t,
           fy, hx, hy, rhs, psi, sx, fwx, sy, fwy,
           pm, pv, xm_out, xm_in, xv_out, xv_in, xr_out, xr_in,
           ym_out, ym_in, yv_out, yv_in, yr_out, yr_in, xmat, ymat, cmat,
           load_s, halo_ss, halo_rs, pair_ss, pair_rs, xm_ss, xm_rs, xv_ss, xv_rs, xr_ss, xr_rs,
           ym_ss, ym_rs, yv_ss, yv_rs, yr_ss, yr_rs):
    px, py = lax.axis_index("px"), lax.axis_index("py")
    core, chip, z = lax.rem(px, 2), lax.div(px, 2), lax.div(py, IN_Z)
    partner = px + 1 - 2 * core

    def owner_of(r):
        return IN_Z * r + lax.rem(2 * core + r, IN_Z)

    is_owner = py == owner_of(z)

    mine = slice(2 * CY, 2 * CY + ROWS)

    def load(k, src, dst):
        return pltpu.make_async_copy(src, dst, load_s.at[k])

    padded = (slice(None), slice(None), slice(0, CY))
    in_xl, in_xu, in_field = load(0, xl, xl_v), load(1, xu, xu_v), load(2, field, fx.at[:, mine, :])
    in_yl, in_yu, in_yi = load(3, yl, yl_v.at[padded]), load(4, yu, yu_v.at[padded]), load(5, yi, yi_v.at[padded])
    in_fo, in_xi = load(6, forcing, fo), load(7, xi, xi_v)
    for c in (in_xl, in_xu, in_field):
        c.start()

    barrier = pltpu.get_barrier_semaphore()

    for dz in (4, 3, 5, 2, 6, 1, 7, 0):
        for dy in (2, 1, 3, 0):
            if dz or dy:
                other = IN_Z * lax.rem(z + dz, NPZ) + lax.rem(py + dy, IN_Z)
                pl.semaphore_signal(barrier, inc=1, device_id=(px, other), device_id_type=MESH)
    for k in (4, 5, 3, 2, 6, 1, 7):
        pl.semaphore_signal(barrier, inc=1, device_id=(lax.rem(px + k, NPX), py), device_id_type=MESH)

    def x_rows(i, h):
        return pl.ds(pl.multiple_of(CY * i + 8 * h, 8), 8)

    def y_rows(j):
        return pl.ds(j, 8, stride=CY)

    def turned(ref, j):
        return ref.reshape(E, CX * YP, 128)[:, pl.ds(j, 8, stride=YP), :].reshape(V, V, 8, 128)

    def x_block(ref):
        return lambda i, h: block(ref, x_rows(i, h))

    def y_block(ref):
        return lambda j, _=0: ref[j]

    def at(ref, k, size, pitch=None):
        return ref.at[pl.ds(pl.multiple_of(k * (pitch or size), 8), size), :]

    def x_copy(src, dst, ss, rs, size, c):
        return pltpu.make_async_remote_copy(
            at(src, c, size), at(dst, chip, size), ss.at[c], rs.at[chip],
            device_id=(2 * c + core, py), device_id_type=MESH)

    def other_chip(k):
        return lax.rem(chip + k, CHIPS)

    def x_send(src, dst, ss, rs, size):
        for k in (2, 1, 3):
            x_copy(src, dst, ss, rs, size, other_chip(k)).start()
        pltpu.make_async_copy(at(src, chip, size), at(dst, chip, size), rs.at[chip]).start()

    def x_sent(src, dst, ss, rs, size):
        for k in range(1, CHIPS):
            x_copy(src, dst, ss, rs, size, other_chip(k)).wait_send()

    def x_back(k):
        d = 2 * other_chip(k // 2) + lax.rem(core + k, 2)
        return pltpu.make_async_remote_copy(
            at(xr_out, lax.div(d, 2), XO * XV), at(xr_in, CHIPS * core + chip, XO * XV), xr_ss.at[d],
            xr_rs.at[CHIPS * core + chip], device_id=(d, py), device_id_type=MESH)

    def pair_copy(k, ref):
        return pltpu.make_async_remote_copy(
            ref, ref, pair_ss.at[k], pair_rs.at[k], device_id=(partner, py), device_id_type=MESH)

    pairs = [pair_copy(0, pm.at[core, 1 - core]), pair_copy(1, pm.at[core, core]), pair_copy(2, pv.at[core])]

    def received(dst, rs, size, count, pitch=None):
        def one(k, _):
            pltpu.make_async_copy(at(dst, k, size, pitch), at(dst, k, size, pitch), rs.at[k]).wait()
            return 0

        lax.fori_loop(0, count, one, 0)

    def slot(d):
        return NPZ * lax.rem(d, IN_Z) + lax.div(d, IN_Z)

    def y_copy(src, dst, ss, rs, size, pitch, r):
        return pltpu.make_async_remote_copy(
            at(src, r, size, pitch), at(dst, slot(py), size, pitch), ss.at[r], rs.at[slot(py)],
            device_id=(px, owner_of(r)), device_id_type=MESH)

    def y_send(src, dst, ss, rs, size, pitch):
        for k in (4, 3, 5, 2, 6, 1, 7):
            y_copy(src, dst, ss, rs, size, pitch, lax.rem(z + k, NPZ)).start()

        @pl.when(is_owner)
        def _():
            pltpu.make_async_copy(at(src, z, size, pitch), at(dst, slot(py), size, pitch), rs.at[slot(py)]).start()

        @pl.when(jnp.logical_not(is_owner))
        def _():
            y_copy(src, dst, ss, rs, size, pitch, z).start()

    def y_sent(src, dst, ss, rs, size, pitch):
        @pl.when(jnp.logical_not(is_owner))
        def _():
            y_copy(src, dst, ss, rs, size, pitch, z).wait_send()

        def one(k, _):
            y_copy(src, dst, ss, rs, size, pitch, lax.rem(z + k, NPZ)).wait_send()
            return 0

        lax.fori_loop(1, NPZ, one, 0)

    xm = (xm_out, xm_in, xm_ss, xm_rs, XO * XM)
    xv = (xv_out, xv_in, xv_ss, xv_rs, XO * XV)
    ym = (ym_out, ym_in, ym_ss, ym_rs, YM, YMP)
    yv = (yv_out, yv_in, yv_ss, yv_rs, YV, YVP)
    in_field.wait()

    def turn(j, _):
        fy[2 + j] = fx[:, pl.ds(2 * CY + j, 8, stride=CY), :]
        return 0

    lax.fori_loop(0, CY, turn, 0)

    right, left = lax.rem(px + 1, NPX), lax.rem(px + NPX - 1, NPX)
    north, south = lax.rem(py + 1, NPY), lax.rem(py + NPY - 1, NPY)
    halos = [
        pltpu.make_async_remote_copy(a, b, halo_ss.at[k], halo_rs.at[k], device_id=d, device_id_type=MESH)
        for k, (a, b, d) in enumerate([
            (fx.at[:, ROWS : ROWS + 2 * CY, :], hx.at[0], (right, py)),
            (fx.at[:, 2 * CY : 4 * CY, :], hx.at[1], (left, py)),
            (fy.at[CY : CY + 2], hy.at[0], (px, north)),
            (fy.at[2:4], hy.at[1], (px, south))])
    ]
    in_xl.wait()
    in_yl.start()
    in_yu.start()
    for first, h in ((True, 1 - core), (False, core)):
        def emit(base, m, h=h):
            pm[core, h, pl.ds(base, E)] = m.reshape(E, 8, 128)

        def before_up(first=first):
            if first:
                in_xu.wait()
                for c in (in_fo, in_xi, in_yi):
                    c.start()

        lo, up = [lambda i, ref=ref, h=h: block(ref, x_rows(i, h)) for ref in (xl_v, xu_v)]
        device_products(lo, up, up, CX, psi, emit, before_up)
        if first:
            pl.semaphore_wait(barrier, NPX + NPY - 2)
            pairs[0].start()
            for c in halos:
                c.start()
        else:
            pairs[1].start()

    in_yl.wait()

    def emit_y(base, m):
        for e in range(E):
            ym_out[pl.ds(base + e, 8, stride=YMP), :] = m[e // V, e % V]

    def lo_y(j):
        m = turned(yl_v, j)
        yl_t[j] = m
        return m

    def up_y(j):
        m = turned(yu_v, j)
        yu_t[j] = m
        return m

    device_products(lo_y, up_y, y_block(yu_t), CY, psi, emit_y, in_yu.wait)
    y_send(*ym)

    pairs[0].wait()

    def half(d, k):
        return pm[d, core, pl.ds(k * E, E)].reshape(V, V, 8, 128)

    def emit_x(base, m):
        for e in range(E):
            xm_out[pl.ds(base + e, 8, stride=XM), :] = m[e // V, e % V]

    m0, n0 = half(0, 0), half(0, 2)
    emit_x(0, product(half(1, 0), m0))
    emit_x(E, half(0, 1) + product(n0, product(half(1, 1), m0)))
    emit_x(2 * E, product(n0, half(1, 2)))
    x_send(*xm)

    in_fo.wait()
    for c in halos:
        c.wait()
    fx[:, 0 : 2 * CY, :] = jnp.where(px == 0, 0.0, hx[0])
    fx[:, 2 * CY + ROWS :, :] = jnp.where(px == NPX - 1, 0.0, hx[1])
    fy[0:2] = jnp.where(py == 0, 0.0, hy[0])
    fy[CY + 2 :] = jnp.where(py == NPY - 1, 0.0, hy[1])

    def difference(v):
        return v[0] - 4.0 * v[1] + 6.0 * v[2] - 4.0 * v[3] + v[4]

    def along_y(j, _):
        d = difference([fy[j + k] for k in range(5)])
        rhs[:, y_rows(j), :] = fo[:, y_rows(j), :] - DISSIPATION * d
        return 0

    lax.fori_loop(0, CY, along_y, 0)
    in_xi.wait()

    def x_source(i, h):
        d = difference([fx[:, x_rows(i + k, h), :] for k in range(5)])
        s = apply(block(xi_v, x_rows(i, h)), rhs[:, x_rows(i, h), :] - DISSIPATION * d)
        sx[:, x_rows(i, h), :] = s
        return s

    def save_fwx(i, h, f):
        fwx[:, x_rows(i, h), :] = f

    def load_fwx(i, h):
        return fwx[:, x_rows(i, h), :]

    ends = forward_cells(x_source, x_block(xl_v), CX, (None, None), save_fwx)
    starts = backward_cells(load_fwx, x_block(xu_v), CX, (None, None), None)
    for h in range(2):
        pv[core, h, pl.ds(0, V)] = ends[h]
        pv[core, h, pl.ds(V, V)] = starts[h]
    pairs[2].start()

    pairs[2].wait()

    def part(d, h, k):
        return pv[d, h, pl.ds(k * V, V)]

    v0 = part(0, core, 0)
    v = part(1, core, 0) + apply(half(1, 0), v0)
    w = part(0, core, 1) + apply(half(0, 2), part(1, core, 1) - apply(half(1, 1), v0))
    for c in range(V):
        xv_out[pl.ds(c, 8, stride=XV), :] = v[c]
        xv_out[pl.ds(V + c, 8, stride=XV), :] = w[c]
    x_send(*xv)

    place = lax.broadcasted_iota(jnp.int32, (V, 8, 128), 1)

    def chain(m, v, by, count):
        def one(_, a):
            return tuple(jnp.where(place < by, 0.0, pltpu.roll(vk + apply(mk(), ak), by, axis=1))
                         for vk, mk, ak in zip(v, m, a))

        return lax.fori_loop(0, count, one, tuple(jnp.zeros((V, 8, 128), F32) for _ in v), unroll=True)

    def chain_back(m, v, by, count):
        def one(_, b):
            return tuple(jnp.where(place >= 8 - by, 0.0, pltpu.roll(vk + apply(mk(), bk), 8 - by, axis=1))
                         for vk, mk, bk in zip(v, m, b))

        return lax.fori_loop(0, count, one, tuple(jnp.zeros((V, 8, 128), F32) for _ in v), unroll=True)

    def held(ref, *at_):
        return lambda: ref[at_].reshape(V, V, 8, 128)

    in_yi.wait()

    def turn_yi(j, _):
        yi_t[j] = turned(yi_v, j)
        return 0

    lax.fori_loop(0, CY, turn_yi, 0)

    received(xm_in, xm_rs, XO * XM, CHIPS)
    for e in range(3 * E):
        xmat[e // E, e % E] = xm_in[pl.ds(e, 8, stride=XM), :]
    received(xv_in, xv_rs, XO * XV, CHIPS)

    def rows_of(ref, first, stride):
        return jnp.stack([ref[pl.ds(first + c, 8, stride=stride), :] for c in range(V)])

    a, = chain([held(xmat, 0)], [rows_of(xv_in, 0, XV)], XO, CHIPS - 1)
    b, = chain_back([held(xmat, 2)], [rows_of(xv_in, V, XV) - apply(held(xmat, 1)(), a)], XO, CHIPS - 1)
    for c in range(V):
        xr_out[pl.ds(c, 8, stride=XV), :] = a[c]
        xr_out[pl.ds(V + c, 8, stride=XV), :] = b[c]
    own = CHIPS * core + chip
    pltpu.make_async_copy(at(xr_out, chip, XO * XV), at(xr_in, own, XO * XV), xr_rs.at[own]).start()
    for k in (4, 5, 2, 3, 6, 7, 1):
        x_back(k).start()
    pairs[1].wait()
    received(xr_in, xr_rs, XO * XV, NPX)

    before, after = [], []
    for h in range(2):
        a, b = rows_of(xr_in, 8 * h * XV, XV), rows_of(xr_in, 8 * h * XV + V, XV)

        def of(d, k, h=h):
            return pm[d, h, pl.ds(k * E, E)].reshape(V, V, 8, 128)

        a1 = part(0, h, 0) + apply(of(0, 0), a)
        b0 = part(1, h, 1) - apply(of(1, 1), a1) + apply(of(1, 2), b)
        before.append(jnp.where(core == 0, a, a1))
        after.append(jnp.where(core == 0, b0, b))

    def load_sx(i, h):
        return sx[:, x_rows(i, h), :]

    forward_cells(load_sx, x_block(xl_v), CX, tuple(before), save_fwx)
    backward_cells(load_fwx, x_block(xu_v), CX, tuple(after), save_fwx)

    def y_source(j, _):
        s = apply(yi_t[j], fwx[:, y_rows(j), :])
        sy[j] = s
        return s

    def save_fwy(j, _, f):
        fwy[j] = f

    def load_fwy(j, _):
        return fwy[j]

    end, = forward_cells(y_source, y_block(yl_t), CY, (None,), save_fwy)
    start, = backward_cells(load_fwy, y_block(yu_t), CY, (None,), None)
    for c in range(V):
        yv_out[pl.ds(c, 8, stride=YVP), :] = end[c]
        yv_out[pl.ds(V + c, 8, stride=YVP), :] = start[c]
    y_send(*yv)

    def y_back(d):
        return pltpu.make_async_remote_copy(
            at(yr_out, slot(d), YV, YVP), at(yr_in, z, YV, YVP), yr_ss.at[d], yr_rs.at[z], device_id=(px, d), device_id_type=MESH)

    @pl.when(is_owner)
    def _():
        received(ym_in, ym_rs, YM, NPY, YMP)
        for d in range(IN_Z):
            for e in range(3 * E):
                ymat[d, e // E, e % E] = ym_in[pl.ds(d * NPZ * YMP + e, 8, stride=YMP), :]
        mm, mz, mn = [[held(ymat, d, k) for d in range(IN_Z)] for k in range(3)]

        def keep(k, m):
            cmat[k] = m.reshape(E, 8, 128)

        phi = mm[0]()
        x = []
        for d in range(1, IN_Z):
            keep(3 + d, product(mz[d](), phi))
            phi = product(mm[d](), phi)
        keep(0, phi)
        x = held(cmat, 3 + IN_Z - 1)()
        for d in range(IN_Z - 2, 0, -1):
            x = held(cmat, 3 + d)() + product(mn[d](), x)
        keep(1, mz[0]() + product(mn[0](), x))
        n = mn[IN_Z - 1]()
        for d in range(IN_Z - 2, -1, -1):
            n = product(mn[d](), n)
        keep(2, n)

        received(yv_in, yv_rs, YV, NPY, YVP)
        v = [rows_of(yv_in, d * NPZ * YVP, YVP) for d in range(IN_Z)]
        w = [rows_of(yv_in, d * NPZ * YVP + V, YVP) for d in range(IN_Z)]
        e = v[0]
        ins = [None]
        for d in range(1, IN_Z):
            ins.append(e)
            e = v[d] + apply(mm[d](), e)
        g = w[IN_Z - 1] - apply(mz[IN_Z - 1](), ins[IN_Z - 1])
        for d in range(IN_Z - 2, -1, -1):
            g = w[d] + apply(mn[d](), g)
            if d:
                g = g - apply(mz[d](), ins[d])
        a, = chain([held(cmat, 0)], [e], 1, NPZ - 1)
        g = g - apply(held(cmat, 1)(), a)
        b, = chain_back([held(cmat, 2)], [g], 1, NPZ - 1)
        ins = [a]
        for d in range(IN_Z - 1):
            ins.append(v[d] + apply(mm[d](), ins[d]))
        ahead = [None] * IN_Z
        ahead[IN_Z - 1] = b
        for d in range(IN_Z - 1, 0, -1):
            ahead[d - 1] = w[d] - apply(mz[d](), ins[d]) + apply(mn[d](), ahead[d])
        for d in range(IN_Z):
            for c in range(V):
                yr_out[pl.ds(d * NPZ * YVP + c, 8, stride=YVP), :] = ins[d][c]
                yr_out[pl.ds(d * NPZ * YVP + V + c, 8, stride=YVP), :] = ahead[d][c]

        for dz in (4, 3, 5, 2, 6, 1, 7, 0):
            for dy in (2, 1, 3, 0):
                if dz or dy:
                    y_back(IN_Z * lax.rem(z + dz, NPZ) + lax.rem(py + dy, IN_Z)).start()
        pltpu.make_async_copy(at(yr_out, slot(py), YV, YVP), at(yr_in, z, YV, YVP), yr_rs.at[z]).start()

    x_sent(*xm)
    x_sent(*xv)
    for k in range(1, NPX):
        x_back(k).wait_send()
    y_sent(*ym)
    y_sent(*yv)

    @pl.when(is_owner)
    def _():
        def one(k, _):
            y_back(lax.rem(py + k, NPY)).wait_send()
            return 0

        lax.fori_loop(1, NPY, one, 0)

    received(yr_in, yr_rs, YV, NPZ, YVP)

    def load_sy(j, _):
        return sy[j]

    def save_res(j, _, u):
        out[:, y_rows(j), :] = u

    forward_cells(load_sy, y_block(yl_t), CY, (rows_of(yr_in, 0, YVP),), save_fwy)
    backward_cells(load_fwy, y_block(yu_t), CY, (rows_of(yr_in, V, YVP),), save_res)


def per_device(field, forcing, *blocks):
    shape = field.shape
    args = [v.reshape(V, ROWS, 128) for v in (field, forcing)] + [m.reshape(E, ROWS, 128) for m in blocks[:3]]
    args += [m.reshape(E, CX, CY, 128) for m in blocks[3:]]

    def vmem(*dims):
        return pltpu.VMEM(dims, F32)

    def dma(n):
        return pltpu.SemaphoreType.DMA((n,))

    scratch = [
        vmem(V, ROWS + 4 * CY, 128), vmem(V, ROWS, 128), *[vmem(E, ROWS, 128) for _ in range(3)],
        *[vmem(E, CX, YP, 128) for _ in range(3)], *[vmem(CY, V, V, 8, 128) for _ in range(3)],
        vmem(CY + 4, V, 8, 128), vmem(2, V, 2 * CY, 128), vmem(2, 2, V, 8, 128), vmem(V, ROWS, 128),
        vmem(CY, V, V, 8, 128), vmem(V, ROWS, 128), vmem(V, ROWS, 128), vmem(CY, V, 8, 128), vmem(CY, V, 8, 128),
        vmem(2, 2, 3 * E, 8, 128), vmem(2, 2, 2 * V, 8, 128), vmem(8 * XM, 128), vmem(8 * XM, 128),
        vmem(8 * XV, 128), vmem(8 * XV, 128), vmem(8 * XV, 128), vmem(CY * XV, 128),
        vmem(CX * YMP, 128), vmem(NPY * YMP, 128),
        vmem(CX * YVP, 128), vmem(NPY * YVP, 128), vmem(NPY * YVP, 128), vmem(CX * YVP, 128),
        vmem(3, E, 8, 128), vmem(IN_Z, 3, E, 8, 128), vmem(3 + IN_Z, E, 8, 128),
        dma(8), dma(4), dma(4), dma(3), dma(3), dma(CHIPS), dma(CHIPS), dma(CHIPS), dma(CHIPS), dma(NPX), dma(NPX),
        dma(NPZ), dma(NPY), dma(NPZ), dma(NPY), dma(NPY), dma(NPZ),
    ]
    result = pl.pallas_call(
        kernel,
        out_shape=jax.ShapeDtypeStruct((V, ROWS, 128), F32),
        in_specs=[pl.BlockSpec(memory_space=pltpu.HBM)] * 8,
        out_specs=pl.BlockSpec(memory_space=pltpu.VMEM),
        scratch_shapes=scratch,
        compiler_params=pltpu.CompilerParams(collective_id=0, has_side_effects=True, vmem_limit_bytes=56000000),
        name="adi",
    )(*args)
    return result.reshape(shape)


def solution(mesh):
    vector, matrix = P(None, "px", "py", None), P(None, None, "px", "py", None)
    return jax.shard_map(
        per_device, mesh=mesh, in_specs=(vector,) * 2 + (matrix,) * 6, out_specs=vector, check_vma=False
    )
```
